32 devices in a mesh: path: 16 (over z, x, core), row: 2 (over y).
Axes of the slice: x: 2, y: 2, z: 4, core: 2. Of those that a mesh axis runs over, the one named last changes fastest.
Arguments:
- main_field: bfloat16 [2, 36, 512, 512], P(None, None, 'path', 'row'), may hold values from -6 to 6
- reflect: float32 [9], replicated, may hold values from 0.5 to 1
- curvature: float32 [9], replicated, may hold values from 100 to 1000
- position: float32 [9], replicated, may hold values from 0 to 1
- wave: float32 [4], replicated, may hold values from 0.8 to 1.6
- ghost_pair: int32 [16, 2], replicated, may hold values from 0 to 8, as said below
- ghost_case: int32 [16], replicated, may hold values from 0 to 3, as said below
Outputs:
- glare: float32 [4, 512, 512], P(None, 'path', 'row')
The draws below stay inside these ranges and needn't reach their ends.
Inputs may be any that keep to these rules, and one draw needn't show every extreme that they name: `ghost_pair`: column 0 is the start surface a and column 1 the turning surface b of a ghost path, with b < a; the triples (a, b, ghost_case) of all ghost paths are distinct. `ghost_case`: together with ghost_pair, no triple (start surface, turning surface, case) appears twice.
All inputs are finite; a program needn't handle non-finite values.
Results may differ from the reference program's by a relative error of at most 0.0003.
Values may be sent and summed in bfloat16 or wider, within the bound.
A program may use at most 128 MiB of HBM per device.

```python
import jax
import jax.numpy as jnp
from jax import lax

NG = 512
CASES = 4
SURF = 9
GHOSTS = 16
FIELDS = 36


def ghost_triples(key):
    pair_count = SURF * (SURF - 1) // 2
    total_count = CASES * pair_count
    order = jax.random.permutation(jax.random.fold_in(key, 7), total_count).astype(jnp.int32)
    last_pair = (SURF - 1) * (SURF - 2) // 2
    first_target = (CASES - 1) * pair_count + last_pair
    order = jnp.where(order == first_target, order[0], order)
    order = order.at[0].set(first_target)
    second_target = 0
    order = jnp.where(order == second_target, order[1], order)
    order = order.at[1].set(second_target)
    chosen = order[:GHOSTS]
    rows_list, cols_list = jnp.tril_indices(SURF, -1)
    pair_index = chosen % pair_count
    case_index = chosen // pair_count
    start_surface = rows_list.astype(jnp.int32)[pair_index]
    turn_surface = cols_list.astype(jnp.int32)[pair_index]
    return (start_surface, turn_surface, case_index)


def draw_ghost_pair(key, part):
    start_surface, turn_surface, case_index = ghost_triples(key)
    return jnp.stack([start_surface, turn_surface], 1).astype(jnp.int32)


def draw_ghost_case(key, part):
    start_surface, turn_surface, case_index = ghost_triples(key)
    return case_index.astype(jnp.int32)


def block_scale(own_key, extent, split, low, high):
    gain = 1.0
    for dim, shards_of in split:
        steps = jax.random.uniform(jax.random.fold_in(jax.random.fold_in(own_key, 6), dim), (shards_of,), jnp.float32, low / len(split), high / len(split))
        gain = gain * jnp.repeat(jnp.exp(steps), extent[dim] // shards_of).reshape((-1,) + (1,) * (len(extent) - 1 - dim))
    return gain


def gaussian(stream_key, dims, spread, reach, cuts=(), kind=jnp.bfloat16):
    array = jax.random.normal(stream_key, dims, jnp.float32) * spread
    if len(cuts) > 0:
        array = block_scale(stream_key, dims, cuts, -0.22, 0.18) * array
    return jnp.clip(array, min=-reach, max=reach).astype(kind)


def setup_inputs(seed: int = 0) -> dict:
    seeds = jax.random.split(jax.random.key(seed), 8)
    return {
        "main_field": gaussian(seeds[0], (2, FIELDS, NG, NG), 1.0, 6.0, ((2, 16), (3, 2))),
        "reflect": jnp.clip(jax.random.uniform(seeds[1], (SURF,), jnp.float32, 0.5, 1.0), 0.5, 1.0),
        "curvature": jnp.clip(jax.random.uniform(seeds[2], (SURF,), jnp.float32, 100.0, 1000.0), 100.0, 1000.0),
        "position": jnp.clip(jax.random.uniform(seeds[3], (SURF,), jnp.float32, 0.0, 1.0), 0.0, 1.0),
        "wave": jnp.clip(jax.random.uniform(seeds[4], (CASES,), jnp.float32, 0.8, 1.6), 0.8, 1.6),
        "ghost_pair": draw_ghost_pair(jax.random.fold_in(seeds[7], 71), 0),
        "ghost_case": draw_ghost_case(jax.random.fold_in(seeds[7], 71), 0),
    }


spread_scale = 2000.0


def reference(main_field, reflect, curvature, position, wave, ghost_pair, ghost_case):
    counter = jnp.arange(NG, dtype=jnp.int32)
    shifted = ((counter + NG // 2) % NG - NG // 2).astype(jnp.float32)
    squares = shifted * shifted
    frequency = (squares[:, None] + squares[None, :]) / float(NG * NG)
    centred = (counter - NG // 2).astype(jnp.float32) / float(NG)
    radial = centred[:, None] * centred[:, None] + centred[None, :] * centred[None, :]
    case_ids = jnp.arange(CASES, dtype=jnp.int32)

    def accumulate(total, ghost):
        start_surf = ghost_pair[ghost, 0]
        turn_surf = ghost_pair[ghost, 1]
        case_id = ghost_case[ghost]
        field_id = case_id * SURF + start_surf
        real_part = main_field[0, field_id].astype(jnp.float32)
        imag_part = main_field[1, field_id].astype(jnp.float32)
        start = lax.complex(reflect[start_surf] * real_part, reflect[start_surf] * imag_part)
        coefficient = spread_scale * wave[case_id] * (position[start_surf] - position[turn_surf])
        phase = coefficient * frequency
        transfer = lax.complex(jnp.cos(phase), -jnp.sin(phase))
        first_hop = jnp.fft.ifft2(transfer * jnp.fft.fft2(start))
        screen = curvature[turn_surf] * radial
        turned = lax.complex(reflect[turn_surf] * jnp.cos(screen), reflect[turn_surf] * jnp.sin(screen)) * first_hop
        second_hop = jnp.fft.ifft2(transfer * jnp.fft.fft2(turned))
        intensity = jnp.real(second_hop) ** 2 + jnp.imag(second_hop) ** 2
        one_hot = (case_ids == case_id).astype(jnp.float32)
        return total + one_hot[:, None, None] * intensity[None], None

    initial = jnp.zeros((CASES, NG, NG), jnp.float32)
    total, _ = lax.scan(accumulate, initial, jnp.arange(GHOSTS, dtype=jnp.int32))
    return total * (CASES / GHOSTS)
```

```python
import functools

import jax
import jax.numpy as jnp
import numpy as np
from jax import lax
from jax.experimental import pallas as pl
from jax.experimental.pallas import tpu as pltpu
from jax.sharding import PartitionSpec as P

CASES = 4
SURF = 9

spread_scale = 2000.0
PARTS = 4
TOP = 32767.0
TINY = 1e-30
SEND = ((2,3,1,0),(2,3,0,1),(0,1,3,2),(0,1,2,3))
ARRIVE = ((0,1,2,3),(1,0,2,3),(2,3,1,0),(3,2,1,0))
BACK = ((0,1,2,3),)*4
ST = set("pass,build,first,second,back,side".split(","))

BF16 = jnp.bfloat16
F32 = jnp.float32
MESH = pl.DeviceIdType.MESH
SMEM = pl.BlockSpec(memory_space=pltpu.SMEM)
VMEM = pl.BlockSpec(memory_space=pltpu.VMEM)

TURN = 2.0 * np.pi
TURN_1 = float(np.float32(6.28125))
TURN_2 = float(np.float32(TURN - 6.28125))


def halves(values):
    high = values.astype(BF16)
    return high, (values - high.astype(F32)).astype(BF16)


def cosine_table(cells):
    counter = np.arange(cells, dtype=np.int64)
    exact = np.cos(TURN / cells * (counter[:, None] * counter[None, :] % cells)) / cells
    high = exact.astype(np.float32).astype(jnp.bfloat16)
    low = (exact - high.astype(np.float64)).astype(np.float32).astype(jnp.bfloat16)
    return np.stack([high, low])


def dot(left, right):
    return jnp.dot(left, right, preferred_element_type=F32)


def dot3(left_high, left_low, right_high, right_low):
    return dot(left_high, right_high) + dot(left_high, right_low) + dot(left_low, right_high)


def cos_sin(phase):
    turns = jnp.floor(phase * (1.0 / TURN) + 0.5)
    rest = (phase - turns * TURN_1) - turns * TURN_2
    return jnp.cos(rest), jnp.sin(rest)


def ghost_scalars(reflect, curvature, position, wave, pair, case, ghost):
    start, turn = pair[0, ghost], pair[1, ghost]
    coefficient = spread_scale * wave[case[ghost]] * (position[start] - position[turn])
    return coefficient, curvature[turn], reflect[start] * reflect[turn]


def build_operator(cells, coefficient, power, table, spread, screened, both):
    counter = lax.broadcasted_iota(jnp.int32, (16, cells), 1)
    row = lax.broadcasted_iota(jnp.int32, (16, cells), 0)
    shifted = ((counter + cells // 2) % cells - cells // 2).astype(F32)
    cosine, sine = cos_sin(coefficient * (shifted * shifted / float(cells * cells)))
    transfer = jnp.where(row == 0, cosine, jnp.where(row == 1, -sine, 0.0))
    high, low = halves(transfer)
    kernel_rows = dot3(high, low, table[0], table[1])
    centred = (counter - cells // 2).astype(F32) / float(cells)
    screen_cos, screen_sin = cos_sin(power * (centred * centred))
    screen_cos, screen_sin = screen_cos[0:1], screen_sin[0:1]
    step = 128
    for begin in range(0, cells, step):
        rows = pl.ds(begin, step)
        real, imag = (
            pltpu.roll(
                jnp.broadcast_to(kernel_rows[part : part + 1], (step, cells)),
                begin, 1, stride=1, stride_axis=0,
            )
            for part in (0, 1)
        )
        spread[0, rows, :], spread[1, rows, :] = halves(real)
        spread[2, rows, :], spread[3, rows, :] = halves(imag)
        screened[0, rows, :], screened[1, rows, :] = halves(real * screen_cos - imag * screen_sin)
        screened[2, rows, :], screened[3, rows, :] = halves(real * screen_sin + imag * screen_cos)

    wide = cells // 2

    @pl.loop(0, 2)
    def _(chunk):
        rows = pl.ds(pl.multiple_of(chunk * wide, wide), wide)
        left = [screened[k, rows, :] for k in range(4)]
        right = [spread[k] for k in range(4)]
        real = dot3(left[0], left[1], right[0], right[1]) - dot3(left[2], left[3], right[2], right[3])
        both[0, rows, :], both[1, rows, :] = halves(real)
        imag = dot3(left[0], left[1], right[2], right[3]) + dot3(left[2], left[3], right[0], right[1])
        both[2, rows, :], both[3, rows, :] = halves(imag)


def slab_first(real, imag, slab, both, middle, rows):
    tall = real.shape[0]
    stacked = jnp.concatenate([real, imag], axis=0)
    weights = [both[k, :, slab] for k in range(4)]
    by_real = dot(stacked, weights[0]) + dot(stacked, weights[1])
    by_imag = dot(stacked, weights[2]) + dot(stacked, weights[3])
    middle[0, rows, :], middle[1, rows, :] = halves(by_real[:tall] - by_imag[tall:])
    middle[2, rows, :], middle[3, rows, :] = halves(by_imag[:tall] + by_real[tall:])


def slab_second(both, middle, rows):
    high = jnp.concatenate([both[0, rows, :], both[2, rows, :]], axis=0)
    low = jnp.concatenate([both[1, rows, :], both[3, rows, :]], axis=0)
    tall = high.shape[0] // 2
    by_real = dot3(high, low, middle[0], middle[1])
    by_imag = dot3(high, low, middle[2], middle[3])
    real = by_real[:tall] - by_imag[tall:]
    imag = by_imag[:tall] + by_real[tall:]
    return real * real + imag * imag


def scratch_of(cells, slab_cells):
    return [
        pltpu.VMEM((4, cells, cells), BF16),
        pltpu.VMEM((4, cells, cells), BF16),
        pltpu.VMEM((4, cells, cells), BF16),
        pltpu.VMEM((4, cells, slab_cells), BF16),
    ]


def whole_kernel(
    cells, paths, row_count,
    field_hbm, table_hbm, *rest,
):
    small_hbm, (out, spread, screened, both, middle, field, table, *small), rest = (
        rest[:6], rest[6:19], rest[19:]
    )
    (
        outgoing, held, bright, got, scale, scale_got,
        load_sem, send_sem, recv_sem, pass_send, pass_recv,
        out_send, out_recv, scale_send, scale_recv, ready,
    ) = rest
    reflect, curvature, position, wave, pair, case = small
    path, row = lax.axis_index("path"), lax.axis_index("row")
    chip, slab_id = path // row_count, path % row_count
    own = chip * row_count + row
    ghosts = case.shape[0]
    slab_cells = cells // row_count
    piece = cells // paths
    devices = paths * row_count
    mine = path * row_count + row
    is_home = slab_id == row
    group = paths // PARTS
    tall = cells // PARTS
    plane = path // group

    def order_of(other_path, other_row):
        if isinstance(other_path, int):
            hops = other_path // group + other_path % group // row_count + other_row
        else:
            inside = lax.div(lax.rem(other_path, group), row_count)
            hops = lax.div(other_path, group) + inside + other_row
        return hops * devices + other_path * row_count + other_row

    order = order_of(path, row)
    everyone = [(p, r) for p in range(paths) for r in range(row_count)]

    def plane_at(table, step):
        mine = table[-1][step]
        for other in range(PARTS - 1):
            mine = jnp.where(plane == other, table[other][step], mine)
        return mine

    loads = [
        pltpu.make_async_copy(source, target, load_sem.at[index])
        for index, (source, target) in enumerate(
            zip((field_hbm, table_hbm, *small_hbm), (field, table, *small))
        )
    ]
    for load in loads[2:] + loads[:2]:
        load.start()

    barrier = pltpu.get_barrier_semaphore()

    earlier = 0
    for other in everyone:
        is_later = order_of(*other) > order
        earlier += jnp.where(order_of(*other) < order, 1, 0)

        @pl.when(is_later)
        def _():
            pl.semaphore_signal(barrier, inc=1, device_id=other, device_id_type=MESH)

    @pl.when(earlier > 0)
    def _():
        pl.semaphore_wait(barrier, earlier)

    for other in everyone:
        same_chip = jnp.logical_and(chip == other[0] // row_count, row == other[1])
        sends_here = jnp.logical_or(slab_id == other[1], same_chip)

        @pl.when(jnp.logical_and(sends_here, order_of(*other) < order))
        def _():
            pl.semaphore_signal(ready.at[mine], inc=1, device_id=other, device_id_type=MESH)

    def field_target(ghost):
        return lax.div(ghost, row_count) * row_count + row, lax.rem(ghost, row_count)

    def field_copy(ghost):
        return pltpu.make_async_remote_copy(
            src_ref=outgoing.at[ghost],
            dst_ref=held.at[row, path],
            send_sem=send_sem.at[ghost],
            recv_sem=recv_sem.at[path],
            device_id=field_target(ghost),
            device_id_type=MESH,
        )

    def field_arrival(source):
        return pltpu.make_async_remote_copy(
            src_ref=outgoing.at[0],
            dst_ref=held.at[slab_id, source],
            send_sem=send_sem.at[0],
            recv_sem=recv_sem.at[source],
            device_id=(path, row),
            device_id_type=MESH,
        )

    home_copy = pltpu.make_async_copy(outgoing.at[own], held.at[row, path], recv_sem.at[path])

    for load in loads[2:] + loads[:1]:
        load.wait()

    each = ghosts // PARTS
    turn_of = lax.rem(own, each)

    for step in range(ghosts):
        ghost = plane_at(SEND, step // each) * each + lax.rem(turn_of + step, each)
        index = case[ghost] * SURF + pair[0, ghost]
        outgoing[ghost, 0] = field[0, index]
        outgoing[ghost, 1] = field[1, index]
        target_path, target_row = field_target(ghost)
        away = jnp.logical_or(ghost != own, jnp.logical_not(is_home))

        @pl.when(jnp.logical_and(away, order_of(target_path, target_row) > order))
        def _():
            pl.semaphore_wait(ready.at[target_path * row_count + target_row], 1)

        @pl.when(away)
        def _():
            field_copy(ghost).start()

        @pl.when(jnp.logical_not(away))
        def _():
            home_copy.start()

    for turn in range(1, row_count):
        partner = chip * row_count + lax.rem(slab_id + turn, row_count)

        @pl.when(jnp.logical_and(lax.rem(partner, row_count) != row, order_of(partner, row) > order))
        def _():
            pl.semaphore_wait(ready.at[partner * row_count + row], 1)

    loads[1].wait()
    coefficient, power, gain = ghost_scalars(
        reflect, curvature, position, wave, pair, case, own
    )
    if "build" in ST: build_operator(cells, coefficient, power, table, spread, screened, both)

    def pass_copy(source, turn):
        return pltpu.make_async_remote_copy(
            src_ref=held.at[slab_id, source],
            dst_ref=held.at[slab_id, source],
            send_sem=pass_send.at[turn - 1, source],
            recv_sem=pass_recv.at[turn - 1, source],
            device_id=(chip * row_count + (slab_id + turn) % row_count, row),
            device_id_type=MESH,
        )

    def pass_arrival(source, turn):
        return pltpu.make_async_remote_copy(
            src_ref=held.at[slab_id, source],
            dst_ref=held.at[(slab_id + row_count - turn) % row_count, source],
            send_sem=pass_send.at[turn - 1, source],
            recv_sem=pass_recv.at[turn - 1, source],
            device_id=(path, row),
            device_id_type=MESH,
        )

    slab = pl.ds(pl.multiple_of(slab_id * slab_cells, slab_cells), slab_cells)

    for turned in range(PARTS):
        chunk = plane_at(ARRIVE, turned)

        @pl.loop(0, group)
        def _(step):
            source = chunk * group + (path + step) % group

            @pl.when(jnp.logical_or(source != path, jnp.logical_not(is_home)))
            def _():
                field_arrival(source).wait_recv()

            @pl.when(jnp.logical_and(source == path, is_home))
            def _():
                home_copy.wait()

            if "pass" in ST:
              for turn in range(1, row_count):
                pass_copy(source, turn).start()

        if "pass" in ST:
          @pl.loop(0, group)
          def _(step):
            for turn in range(1, row_count):
                pass_arrival(chunk * group + step, turn).wait_recv()

        def rows_of(part):
            return jnp.concatenate(
                [
                    held[side, pl.ds(chunk * group, group), part].reshape(tall, slab_cells)
                    for side in range(row_count)
                ],
                axis=1,
            )

        if "first" in ST:
          slab_first(
            rows_of(0), rows_of(1), slab, both, middle, pl.ds(pl.multiple_of(chunk * tall, tall), tall)
          )

    def bright_copies(target):
        return [
            pltpu.make_async_remote_copy(
                src_ref=source.at[target],
                dst_ref=arrived.at[own],
                send_sem=sent.at[target],
                recv_sem=received.at[own],
                device_id=(target, slab_id),
                device_id_type=MESH,
            )
            for source, arrived, sent, received in (
                (bright, got, out_send, out_recv),
                (scale, scale_got, scale_send, scale_recv),
            )[:2 if "side" in ST else 1]
        ]

    def bright_arrivals(ghost):
        return [
            pltpu.make_async_remote_copy(
                src_ref=source.at[0],
                dst_ref=arrived.at[ghost],
                send_sem=sent.at[0],
                recv_sem=received.at[ghost],
                device_id=(path, row),
                device_id_type=MESH,
            )
            for source, arrived, sent, received in (
                (bright, got, out_send, out_recv),
                (scale, scale_got, scale_send, scale_recv),
            )[:2 if "side" in ST else 1]
        ]

    home_bright = [
        pltpu.make_async_copy(bright.at[path], got.at[own], out_recv.at[own]),
        pltpu.make_async_copy(scale.at[path], scale_got.at[own], scale_recv.at[own]),
    ]
    unit = gain * gain * (CASES / ghosts / TOP)

    for turned in range(PARTS):
      chunk = plane_at(BACK, turned)
      if "second" in ST:
        rows = pl.ds(pl.multiple_of(chunk * tall, tall), tall)
        intensity = slab_second(both, middle, rows).reshape(group, piece, slab_cells)
        peak = jnp.max(intensity, axis=1, keepdims=True)
        codes = intensity * (TOP / jnp.maximum(peak, TINY)) + 0.5
        bright[pl.ds(chunk * group, group)] = codes.astype(jnp.int32).astype(jnp.int16)
        scale[pl.ds(chunk * group, group)] = peak * unit

      if "back" in ST:
        for step in range(group):
            target = chunk * group + lax.rem(path + step, group)

            @pl.when(jnp.logical_or(target != path, jnp.logical_not(is_home)))
            def _():
                for copy in bright_copies(target):
                    copy.start()

            @pl.when(jnp.logical_and(target == path, is_home))
            def _():
                for copy in home_bright[:2 if "side" in ST else 1]:
                    copy.start()

    out[...] = jnp.zeros_like(out)

    for step in range(ghosts):
        ghost = plane_at(ARRIVE, step // each) * each + lax.rem(turn_of + step, each)

        if "back" in ST:
          @pl.when(jnp.logical_or(ghost != own, jnp.logical_not(is_home)))
          def _():
            for copy in bright_arrivals(ghost):
                copy.wait_recv()

          @pl.when(jnp.logical_and(ghost == own, is_home))
          def _():
            for copy in home_bright[:2 if "side" in ST else 1]:
                copy.wait()

        values = got[ghost].astype(jnp.int32).astype(F32) * scale_got[ghost]
        for index in range(CASES):
            chosen = jnp.where(case[ghost] == index, 1.0, 0.0)
            out[index] += chosen * values

    @pl.loop(0, ghosts)
    def _(ghost):
        @pl.when(jnp.logical_or(ghost != own, jnp.logical_not(is_home)))
        def _():
            field_copy(ghost).wait_send()

    @pl.loop(0, paths)
    def _(source):
        if "pass" in ST:
          for turn in range(1, row_count):
            pass_copy(source, turn).wait_send()

        if "back" in ST:
          @pl.when(jnp.logical_or(source != path, jnp.logical_not(is_home)))
          def _():
            for copy in bright_copies(source):
                copy.wait_send()


def whole(cells, paths, row_count, main_field, table, *small):
    ghosts = small[-1].shape[0]
    piece, slab_cells = cells // paths, cells // row_count
    return pl.pallas_call(
        functools.partial(whole_kernel, cells, paths, row_count),
        out_shape=jax.ShapeDtypeStruct((CASES, piece, slab_cells), F32),
        in_specs=[pl.BlockSpec(memory_space=pltpu.HBM)] * 8,
        out_specs=VMEM,
        scratch_shapes=scratch_of(cells, slab_cells)
        + [
            pltpu.VMEM(main_field.shape, BF16),
            pltpu.VMEM((2, cells, cells), BF16),
            *[pltpu.SMEM(array.shape, array.dtype) for array in small],
            pltpu.VMEM((ghosts, 2, piece, slab_cells), BF16),
            pltpu.VMEM((row_count, paths, 2, piece, slab_cells), BF16),
            pltpu.VMEM((paths, piece, slab_cells), jnp.int16),
            pltpu.VMEM((ghosts, piece, slab_cells), jnp.int16),
            pltpu.VMEM((paths, 1, slab_cells), F32),
            pltpu.VMEM((ghosts, 1, slab_cells), F32),
            pltpu.SemaphoreType.DMA((8,)),
            pltpu.SemaphoreType.DMA((ghosts,)),
            pltpu.SemaphoreType.DMA((paths,)),
            pltpu.SemaphoreType.DMA((row_count - 1, paths)),
            pltpu.SemaphoreType.DMA((row_count - 1, paths)),
            pltpu.SemaphoreType.DMA((paths,)),
            pltpu.SemaphoreType.DMA((ghosts,)),
            pltpu.SemaphoreType.DMA((paths,)),
            pltpu.SemaphoreType.DMA((ghosts,)),
            pltpu.SemaphoreType.REGULAR((paths * row_count,)),
        ],
        compiler_params=pltpu.CompilerParams(
            collective_id=0, has_side_effects=True, vmem_limit_bytes=60 * 1024 * 1024
        ),
    )(main_field, table, *small)


def slab_kernel(
    cells, row_count, field, table, reflect, curvature, position, wave, pair, case, slot, out,
    spread, screened, both, middle,
):
    slab_cells = cells // row_count
    coefficient, power, gain = ghost_scalars(
        reflect, curvature, position, wave, pair, case, slot[0]
    )
    build_operator(cells, coefficient, power, table, spread, screened, both)
    slab = pl.ds(pl.multiple_of(slot[1] * slab_cells, slab_cells), slab_cells)
    tall = cells // 2

    @pl.loop(0, 2)
    def _(chunk):
        rows = pl.ds(pl.multiple_of(chunk * tall, tall), tall)
        slab_first(field[0, rows, :], field[1, rows, :], slab, both, middle, rows)

    @pl.loop(0, 2)
    def _(chunk):
        rows = pl.ds(pl.multiple_of(chunk * tall, tall), tall)
        out[rows, :] = gain * gain * slab_second(both, middle, rows)


def local(main_field, table, *small):
    paths = lax.axis_size("path")
    row_count = lax.axis_size("row")
    piece, slab_cells = main_field.shape[2:]
    cells = piece * paths
    pair, case = small[-2:]
    ghosts = case.shape[0]
    if piece % 16 == 0 and ghosts == paths and paths % (PARTS * row_count) == 0 and row_count > 1:
        return whole(cells, paths, row_count, main_field, table, *small)
    per_device = ghosts // paths
    fields = jnp.arange(main_field.shape[1], dtype=jnp.int32)
    wanted = (fields[None, :] == (case * SURF + pair[0])[:, None]).astype(BF16)
    picked = jnp.einsum(
        "gf,cfrv->cgrv", wanted, main_field, preferred_element_type=F32
    ).astype(BF16)
    picked = picked.reshape(2, paths, per_device, piece, slab_cells)
    arrived = lax.all_to_all(picked, "path", split_axis=1, concat_axis=3, tiled=True)
    fields = lax.all_gather(
        arrived.reshape(2, per_device, cells, slab_cells), "row", axis=3, tiled=True
    )
    bright = []
    for index in range(per_device):
        slot = jnp.stack([lax.axis_index("path") * per_device + index, lax.axis_index("row")])
        bright.append(
            pl.pallas_call(
                functools.partial(slab_kernel, cells, row_count),
                out_shape=jax.ShapeDtypeStruct((cells, slab_cells), F32),
                in_specs=[VMEM, VMEM] + [SMEM] * 7,
                out_specs=VMEM,
                scratch_shapes=scratch_of(cells, slab_cells),
                compiler_params=pltpu.CompilerParams(vmem_limit_bytes=48 * 1024 * 1024),
            )(fields[:, index], table, *small, slot)
        )
    got = lax.all_to_all(jnp.stack(bright), "path", split_axis=1, concat_axis=0, tiled=True)
    got = got.reshape(paths, per_device, piece, slab_cells).reshape(ghosts, piece, slab_cells)
    chosen = (case[:, None] == jnp.arange(CASES, dtype=jnp.int32)).astype(F32)
    total = jnp.sum(chosen[:, :, None, None] * got[:, None], 0)
    return total * (CASES / ghosts)


def solution(mesh):
    in_specs = (P(None, None, "path", "row"), P(), P(), P(), P(), P(), P())
    out_specs = P(None, "path", "row")

    def run(main_field, reflect, curvature, position, wave, pair, case):
        small = (reflect, curvature, position, wave, pair.T, case)
        table = cosine_table(main_field.shape[2] * mesh.shape["path"])
        return local(main_field, jnp.asarray(table), *small)

    return jax.shard_map(run, mesh=mesh, in_specs=in_specs, out_specs=out_specs, check_vma=False)
```

```python
import functools

import jax
import jax.numpy as jnp
import numpy as np
from jax import lax
from jax.experimental import pallas as pl
from jax.experimental.pallas import tpu as pltpu
from jax.sharding import PartitionSpec as P

CASES = 4
SURF = 9

spread_scale = 2000.0
PARTS = 4
TOP = 32767.0
TINY = 1e-30
SEND = ((2,1,0,3),(3,0,1,2),(0,3,2,1),(1,2,3,0))
EARLY = 3
HOLD = 4
AHEAD = 1
ARRIVE = ((0,1,2,3),(1,0,3,2),(2,3,0,1),(3,2,1,0))
BACK = ((2,3,1,0),(2,3,0,1),(0,1,3,2),(0,1,2,3))
ST = set("pass,build,first,second,back,side".split(","))

BF16 = jnp.bfloat16
F32 = jnp.float32
MESH = pl.DeviceIdType.MESH
SMEM = pl.BlockSpec(memory_space=pltpu.SMEM)
VMEM = pl.BlockSpec(memory_space=pltpu.VMEM)

TURN = 2.0 * np.pi
TURN_1 = float(np.float32(6.28125))
TURN_2 = float(np.float32(TURN - 6.28125))


def halves(values):
    high = values.astype(BF16)
    return high, (values - high.astype(F32)).astype(BF16)


def cosine_table(cells):
    counter = np.arange(cells, dtype=np.int64)
    exact = np.cos(TURN / cells * (counter[:, None] * counter[None, :] % cells)) / cells
    high = exact.astype(np.float32).astype(jnp.bfloat16)
    low = (exact - high.astype(np.float64)).astype(np.float32).astype(jnp.bfloat16)
    return np.stack([high, low])


def dot(left, right):
    return jnp.dot(left, right, preferred_element_type=F32)


def dot3(left_high, left_low, right_high, right_low):
    return dot(left_high, right_high) + dot(left_high, right_low) + dot(left_low, right_high)


def cos_sin(phase):
    turns = jnp.floor(phase * (1.0 / TURN) + 0.5)
    rest = (phase - turns * TURN_1) - turns * TURN_2
    return jnp.cos(rest), jnp.sin(rest)


def ghost_scalars(reflect, curvature, position, wave, pair, case, ghost):
    start, turn = pair[0, ghost], pair[1, ghost]
    coefficient = spread_scale * wave[case[ghost]] * (position[start] - position[turn])
    return coefficient, curvature[turn], reflect[start] * reflect[turn]


def build_operator(cells, coefficient, power, table, spread, screened, both):
    counter = lax.broadcasted_iota(jnp.int32, (16, cells), 1)
    row = lax.broadcasted_iota(jnp.int32, (16, cells), 0)
    shifted = ((counter + cells // 2) % cells - cells // 2).astype(F32)
    cosine, sine = cos_sin(coefficient * (shifted * shifted / float(cells * cells)))
    transfer = jnp.where(row == 0, cosine, jnp.where(row == 1, -sine, 0.0))
    high, low = halves(transfer)
    kernel_rows = dot3(high, low, table[0], table[1])
    centred = (counter - cells // 2).astype(F32) / float(cells)
    screen_cos, screen_sin = cos_sin(power * (centred * centred))
    screen_cos, screen_sin = screen_cos[0:1], screen_sin[0:1]
    step = 128
    for begin in range(0, cells, step):
        rows = pl.ds(begin, step)
        real, imag = (
            pltpu.roll(
                jnp.broadcast_to(kernel_rows[part : part + 1], (step, cells)),
                begin, 1, stride=1, stride_axis=0,
            )
            for part in (0, 1)
        )
        spread[0, rows, :], spread[1, rows, :] = halves(real)
        spread[2, rows, :], spread[3, rows, :] = halves(imag)
        screened[0, rows, :], screened[1, rows, :] = halves(real * screen_cos - imag * screen_sin)
        screened[2, rows, :], screened[3, rows, :] = halves(real * screen_sin + imag * screen_cos)

    wide = cells // 2

    @pl.loop(0, 2)
    def _(chunk):
        rows = pl.ds(pl.multiple_of(chunk * wide, wide), wide)
        left = [screened[k, rows, :] for k in range(4)]
        right = [spread[k] for k in range(4)]
        real = dot3(left[0], left[1], right[0], right[1]) - dot3(left[2], left[3], right[2], right[3])
        both[0, rows, :], both[1, rows, :] = halves(real)
        imag = dot3(left[0], left[1], right[2], right[3]) + dot3(left[2], left[3], right[0], right[1])
        both[2, rows, :], both[3, rows, :] = halves(imag)


def slab_first(real, imag, slab, both, middle, rows):
    tall = real.shape[0]
    stacked = jnp.concatenate([real, imag], axis=0)
    weights = [both[k, :, slab] for k in range(4)]
    by_real = dot(stacked, weights[0]) + dot(stacked, weights[1])
    by_imag = dot(stacked, weights[2]) + dot(stacked, weights[3])
    middle[0, rows, :], middle[1, rows, :] = halves(by_real[:tall] - by_imag[tall:])
    middle[2, rows, :], middle[3, rows, :] = halves(by_imag[:tall] + by_real[tall:])


def slab_second(both, middle, rows, depth):
    high = jnp.concatenate([both[0, rows, depth], both[2, rows, depth]], axis=0)
    low = jnp.concatenate([both[1, rows, depth], both[3, rows, depth]], axis=0)
    tall = high.shape[0] // 2
    by_real = dot3(high, low, middle[0, depth, :], middle[1, depth, :])
    by_imag = dot3(high, low, middle[2, depth, :], middle[3, depth, :])
    return by_real[:tall] - by_imag[tall:], by_imag[:tall] + by_real[tall:]


def scratch_of(cells, slab_cells):
    return [
        pltpu.VMEM((4, cells, cells), BF16),
        pltpu.VMEM((4, cells, cells), BF16),
        pltpu.VMEM((4, cells, cells), BF16),
        pltpu.VMEM((4, cells, slab_cells), BF16),
    ]


def whole_kernel(
    cells, paths, row_count,
    field_hbm, table_hbm, *rest,
):
    small_hbm, (out, spread, screened, both, middle, field, table, *small), rest = (
        rest[:6], rest[6:19], rest[19:]
    )
    (
        outgoing, held, partial, bright, got, scale, scale_got,
        load_sem, send_sem, recv_sem, pass_send, pass_recv,
        out_send, out_recv, scale_send, scale_recv, ready,
    ) = rest
    reflect, curvature, position, wave, pair, case = small
    path, row = lax.axis_index("path"), lax.axis_index("row")
    chip, slab_id = path // row_count, path % row_count
    own = chip * row_count + row
    ghosts = case.shape[0]
    slab_cells = cells // row_count
    piece = cells // paths
    devices = paths * row_count
    mine = path * row_count + row
    is_home = slab_id == row
    group = paths // PARTS
    tall = cells // PARTS
    plane = path // group

    def order_of(other_path, other_row):
        if isinstance(other_path, int):
            hops = other_path // group + other_path % group // row_count + other_row
        else:
            inside = lax.div(lax.rem(other_path, group), row_count)
            hops = lax.div(other_path, group) + inside + other_row
        return hops * devices + other_path * row_count + other_row

    order = order_of(path, row)
    everyone = [(p, r) for p in range(paths) for r in range(row_count)]

    def plane_at(table, step):
        mine = table[-1][step]
        for other in range(PARTS - 1):
            mine = jnp.where(plane == other, table[other][step], mine)
        return mine

    loads = [
        pltpu.make_async_copy(source, target, load_sem.at[index])
        for index, (source, target) in enumerate(
            zip((field_hbm, table_hbm, *small_hbm), (field, table, *small))
        )
    ]
    for load in loads[2:] + loads[:2]:
        load.start()

    barrier = pltpu.get_barrier_semaphore()

    earlier = 0
    for other in everyone:
        is_later = order_of(*other) > order
        earlier += jnp.where(order_of(*other) < order, 1, 0)

        @pl.when(is_later)
        def _():
            pl.semaphore_signal(barrier, inc=1, device_id=other, device_id_type=MESH)

    @pl.when(earlier > 0)
    def _():
        pl.semaphore_wait(barrier, earlier)

    for other in everyone:
        same_chip = jnp.logical_and(chip == other[0] // row_count, row == other[1])
        sends_here = jnp.logical_or(slab_id == other[1], same_chip)

        @pl.when(jnp.logical_and(sends_here, order_of(*other) < order))
        def _():
            pl.semaphore_signal(ready.at[mine], inc=1, device_id=other, device_id_type=MESH)

    def field_target(ghost):
        return lax.div(ghost, row_count) * row_count + row, lax.rem(ghost, row_count)

    def field_copy(ghost):
        return pltpu.make_async_remote_copy(
            src_ref=outgoing.at[ghost],
            dst_ref=held.at[row, path],
            send_sem=send_sem.at[ghost],
            recv_sem=recv_sem.at[path],
            device_id=field_target(ghost),
            device_id_type=MESH,
        )

    def field_arrival(source):
        return pltpu.make_async_remote_copy(
            src_ref=outgoing.at[0],
            dst_ref=held.at[slab_id, source],
            send_sem=send_sem.at[0],
            recv_sem=recv_sem.at[source],
            device_id=(path, row),
            device_id_type=MESH,
        )

    home_copy = pltpu.make_async_copy(outgoing.at[own], held.at[row, path], recv_sem.at[path])

    for load in loads[2:] + loads[:1]:
        load.wait()

    each = ghosts // PARTS
    turn_of = lax.rem(own, each)

    def send_plane(step):
        for turn in range(each):
            ghost = plane_at(SEND, step) * each + lax.rem(turn_of + turn, each)
            index = case[ghost] * SURF + pair[0, ghost]
            outgoing[ghost, 0] = field[0, index]
            outgoing[ghost, 1] = field[1, index]
            target_path, target_row = field_target(ghost)
            away = jnp.logical_or(ghost != own, jnp.logical_not(is_home))

            @pl.when(jnp.logical_and(away, order_of(target_path, target_row) > order))
            def _():
                pl.semaphore_wait(ready.at[target_path * row_count + target_row], 1)

            @pl.when(away)
            def _():
                field_copy(ghost).start()

            @pl.when(jnp.logical_not(away))
            def _():
                home_copy.start()

    def drain_plane(step, count):
        for turn in range(*count):
            ghost = plane_at(SEND, step) * each + lax.rem(turn_of + turn, each)

            @pl.when(jnp.logical_or(ghost != own, jnp.logical_not(is_home)))
            def _():
                field_copy(ghost).wait_send()

    for step in range(EARLY):
        send_plane(step)

    for turn in range(1, row_count):
        partner = chip * row_count + lax.rem(slab_id + turn, row_count)

        @pl.when(jnp.logical_and(lax.rem(partner, row_count) != row, order_of(partner, row) > order))
        def _():
            pl.semaphore_wait(ready.at[partner * row_count + row], 1)

    loads[1].wait()
    coefficient, power, gain = ghost_scalars(
        reflect, curvature, position, wave, pair, case, own
    )
    if "build" in ST: build_operator(cells, coefficient, power, table, spread, screened, both)

    drain_plane(0, (0, HOLD))
    for step in range(EARLY, PARTS):
        send_plane(step)

    def pass_copy(source, turn):
        return pltpu.make_async_remote_copy(
            src_ref=held.at[slab_id, source],
            dst_ref=held.at[slab_id, source],
            send_sem=pass_send.at[turn - 1, source],
            recv_sem=pass_recv.at[turn - 1, source],
            device_id=(chip * row_count + (slab_id + turn) % row_count, row),
            device_id_type=MESH,
        )

    def pass_arrival(source, turn):
        return pltpu.make_async_remote_copy(
            src_ref=held.at[slab_id, source],
            dst_ref=held.at[(slab_id + row_count - turn) % row_count, source],
            send_sem=pass_send.at[turn - 1, source],
            recv_sem=pass_recv.at[turn - 1, source],
            device_id=(path, row),
            device_id_type=MESH,
        )

    slab = pl.ds(pl.multiple_of(slab_id * slab_cells, slab_cells), slab_cells)

    def take_plane(step):
        for turn in range(group):
            source = plane_at(ARRIVE, step) * group + lax.rem(path + turn, group)

            @pl.when(jnp.logical_or(source != path, jnp.logical_not(is_home)))
            def _():
                field_arrival(source).wait_recv()

            @pl.when(jnp.logical_and(source == path, is_home))
            def _():
                home_copy.wait()

            if "pass" in ST:
                for other in range(1, row_count):
                    pass_copy(source, other).start()

    def first_plane(step):
        chunk = plane_at(ARRIVE, step)
        if "pass" in ST:
            for turn in range(group):
                for other in range(1, row_count):
                    pass_arrival(chunk * group + turn, other).wait_recv()

        def rows_of(part):
            return jnp.concatenate(
                [
                    held[side, pl.ds(chunk * group, group), part].reshape(tall, slab_cells)
                    for side in range(row_count)
                ],
                axis=1,
            )

        if "first" in ST:
            rows = pl.ds(pl.multiple_of(chunk * tall, tall), tall)
            slab_first(rows_of(0), rows_of(1), slab, both, middle, rows)

    def half_at(index):
        return pl.ds(pl.multiple_of(index * (cells // 2), cells // 2), cells // 2)

    def half_second():
        @pl.loop(0, 2)
        def _(chunk):
            rows = half_at(chunk)
            real, imag = slab_second(both, middle, rows, half_at(plane // 2))
            partial[0, rows, :], partial[1, rows, :] = real, imag

    take_plane(0)
    take_plane(1)
    if AHEAD == 2:
        take_plane(2)
    first_plane(0)
    first_plane(1)
    if AHEAD == 1:
        take_plane(2)
    if "second" in ST: half_second()
    if AHEAD == 0:
        take_plane(2)
    first_plane(2)
    take_plane(3)
    first_plane(3)

    def bright_copies(target):
        return [
            pltpu.make_async_remote_copy(
                src_ref=source.at[target],
                dst_ref=arrived.at[own],
                send_sem=sent.at[target],
                recv_sem=received.at[own],
                device_id=(target, slab_id),
                device_id_type=MESH,
            )
            for source, arrived, sent, received in (
                (bright, got, out_send, out_recv),
                (scale, scale_got, scale_send, scale_recv),
            )[:2 if "side" in ST else 1]
        ]

    def bright_arrivals(ghost):
        return [
            pltpu.make_async_remote_copy(
                src_ref=source.at[0],
                dst_ref=arrived.at[ghost],
                send_sem=sent.at[0],
                recv_sem=received.at[ghost],
                device_id=(path, row),
                device_id_type=MESH,
            )
            for source, arrived, sent, received in (
                (bright, got, out_send, out_recv),
                (scale, scale_got, scale_send, scale_recv),
            )[:2 if "side" in ST else 1]
        ]

    home_bright = [
        pltpu.make_async_copy(bright.at[path], got.at[own], out_recv.at[own]),
        pltpu.make_async_copy(scale.at[path], scale_got.at[own], scale_recv.at[own]),
    ]
    unit = gain * gain * (CASES / ghosts / TOP)

    for turned in range(PARTS):
      chunk = plane_at(BACK, turned)
      if "second" in ST:
        rows = pl.ds(pl.multiple_of(chunk * tall, tall), tall)
        real, imag = slab_second(both, middle, rows, half_at(1 - plane // 2))
        real, imag = real + partial[0, rows, :], imag + partial[1, rows, :]
        intensity = (real * real + imag * imag).reshape(group, piece, slab_cells)
        peak = jnp.max(intensity, axis=1, keepdims=True)
        codes = intensity * (TOP / jnp.maximum(peak, TINY)) + 0.5
        bright[pl.ds(chunk * group, group)] = codes.astype(jnp.int32).astype(jnp.int16)
        scale[pl.ds(chunk * group, group)] = peak * unit

      if "back" in ST:
        for step in range(group):
            target = chunk * group + lax.rem(path + step, group)

            @pl.when(jnp.logical_or(target != path, jnp.logical_not(is_home)))
            def _():
                for copy in bright_copies(target):
                    copy.start()

            @pl.when(jnp.logical_and(target == path, is_home))
            def _():
                for copy in home_bright[:2 if "side" in ST else 1]:
                    copy.start()

    out[...] = jnp.zeros_like(out)

    for step in range(ghosts):
        ghost = plane_at(ARRIVE, step // each) * each + lax.rem(turn_of + step, each)

        if "back" in ST:
          @pl.when(jnp.logical_or(ghost != own, jnp.logical_not(is_home)))
          def _():
            for copy in bright_arrivals(ghost):
                copy.wait_recv()

          @pl.when(jnp.logical_and(ghost == own, is_home))
          def _():
            for copy in home_bright[:2 if "side" in ST else 1]:
                copy.wait()

        values = got[ghost].astype(jnp.int32).astype(F32) * scale_got[ghost]
        for index in range(CASES):
            chosen = jnp.where(case[ghost] == index, 1.0, 0.0)
            out[index] += chosen * values

    drain_plane(0, (HOLD, each))
    for step in range(1, PARTS):
        drain_plane(step, (0, each))

    @pl.loop(0, paths)
    def _(source):
        if "pass" in ST:
          for turn in range(1, row_count):
            pass_copy(source, turn).wait_send()

        if "back" in ST:
          @pl.when(jnp.logical_or(source != path, jnp.logical_not(is_home)))
          def _():
            for copy in bright_copies(source):
                copy.wait_send()


def whole(cells, paths, row_count, main_field, table, *small):
    ghosts = small[-1].shape[0]
    piece, slab_cells = cells // paths, cells // row_count
    return pl.pallas_call(
        functools.partial(whole_kernel, cells, paths, row_count),
        out_shape=jax.ShapeDtypeStruct((CASES, piece, slab_cells), F32),
        in_specs=[pl.BlockSpec(memory_space=pltpu.HBM)] * 8,
        out_specs=VMEM,
        scratch_shapes=scratch_of(cells, slab_cells)
        + [
            pltpu.VMEM(main_field.shape, BF16),
            pltpu.VMEM((2, cells, cells), BF16),
            *[pltpu.SMEM(array.shape, array.dtype) for array in small],
            pltpu.VMEM((ghosts, 2, piece, slab_cells), BF16),
            pltpu.VMEM((row_count, paths, 2, piece, slab_cells), BF16),
            pltpu.VMEM((2, cells, slab_cells), F32),
            pltpu.VMEM((paths, piece, slab_cells), jnp.int16),
            pltpu.VMEM((ghosts, piece, slab_cells), jnp.int16),
            pltpu.VMEM((paths, 1, slab_cells), F32),
            pltpu.VMEM((ghosts, 1, slab_cells), F32),
            pltpu.SemaphoreType.DMA((8,)),
            pltpu.SemaphoreType.DMA((ghosts,)),
            pltpu.SemaphoreType.DMA((paths,)),
            pltpu.SemaphoreType.DMA((row_count - 1, paths)),
            pltpu.SemaphoreType.DMA((row_count - 1, paths)),
            pltpu.SemaphoreType.DMA((paths,)),
            pltpu.SemaphoreType.DMA((ghosts,)),
            pltpu.SemaphoreType.DMA((paths,)),
            pltpu.SemaphoreType.DMA((ghosts,)),
            pltpu.SemaphoreType.REGULAR((paths * row_count,)),
        ],
        compiler_params=pltpu.CompilerParams(
            collective_id=0, has_side_effects=True, vmem_limit_bytes=60 * 1024 * 1024
        ),
    )(main_field, table, *small)


def slab_kernel(
    cells, row_count, field, table, reflect, curvature, position, wave, pair, case, slot, out,
    spread, screened, both, middle,
):
    slab_cells = cells // row_count
    coefficient, power, gain = ghost_scalars(
        reflect, curvature, position, wave, pair, case, slot[0]
    )
    build_operator(cells, coefficient, power, table, spread, screened, both)
    slab = pl.ds(pl.multiple_of(slot[1] * slab_cells, slab_cells), slab_cells)
    tall = cells // 2

    @pl.loop(0, 2)
    def _(chunk):
        rows = pl.ds(pl.multiple_of(chunk * tall, tall), tall)
        slab_first(field[0, rows, :], field[1, rows, :], slab, both, middle, rows)

    @pl.loop(0, 2)
    def _(chunk):
        rows = pl.ds(pl.multiple_of(chunk * tall, tall), tall)
        real, imag = slab_second(both, middle, rows, pl.ds(0, cells))
        out[rows, :] = gain * gain * (real * real + imag * imag)


def local(main_field, table, *small):
    paths = lax.axis_size("path")
    row_count = lax.axis_size("row")
    piece, slab_cells = main_field.shape[2:]
    cells = piece * paths
    pair, case = small[-2:]
    ghosts = case.shape[0]
    if piece % 16 == 0 and ghosts == paths and paths % (PARTS * row_count) == 0 and row_count > 1:
        return whole(cells, paths, row_count, main_field, table, *small)
    per_device = ghosts // paths
    fields = jnp.arange(main_field.shape[1], dtype=jnp.int32)
    wanted = (fields[None, :] == (case * SURF + pair[0])[:, None]).astype(BF16)
    picked = jnp.einsum(
        "gf,cfrv->cgrv", wanted, main_field, preferred_element_type=F32
    ).astype(BF16)
    picked = picked.reshape(2, paths, per_device, piece, slab_cells)
    arrived = lax.all_to_all(picked, "path", split_axis=1, concat_axis=3, tiled=True)
    fields = lax.all_gather(
        arrived.reshape(2, per_device, cells, slab_cells), "row", axis=3, tiled=True
    )
    bright = []
    for index in range(per_device):
        slot = jnp.stack([lax.axis_index("path") * per_device + index, lax.axis_index("row")])
        bright.append(
            pl.pallas_call(
                functools.partial(slab_kernel, cells, row_count),
                out_shape=jax.ShapeDtypeStruct((cells, slab_cells), F32),
                in_specs=[VMEM, VMEM] + [SMEM] * 7,
                out_specs=VMEM,
                scratch_shapes=scratch_of(cells, slab_cells),
                compiler_params=pltpu.CompilerParams(vmem_limit_bytes=48 * 1024 * 1024),
            )(fields[:, index], table, *small, slot)
        )
    got = lax.all_to_all(jnp.stack(bright), "path", split_axis=1, concat_axis=0, tiled=True)
    got = got.reshape(paths, per_device, piece, slab_cells).reshape(ghosts, piece, slab_cells)
    chosen = (case[:, None] == jnp.arange(CASES, dtype=jnp.int32)).astype(F32)
    total = jnp.sum(chosen[:, :, None, None] * got[:, None], 0)
    return total * (CASES / ghosts)


def solution(mesh):
    in_specs = (P(None, None, "path", "row"), P(), P(), P(), P(), P(), P())
    out_specs = P(None, "path", "row")

    def run(main_field, reflect, curvature, position, wave, pair, case):
        small = (reflect, curvature, position, wave, pair.T, case)
        table = cosine_table(main_field.shape[2] * mesh.shape["path"])
        return local(main_field, jnp.asarray(table), *small)

    return jax.shard_map(run, mesh=mesh, in_specs=in_specs, out_specs=out_specs, check_vma=False)
```

```python
import functools
import jax
import jax.numpy as jnp
import numpy as np
from jax import lax
from jax.experimental import pallas as pl
from jax.experimental.pallas import tpu as pltpu
from jax.sharding import PartitionSpec as P
CASES = 4
SURF = 9
spread_scale = 2000.0
PARTS = 4
TOP = 32767.0
TINY = 1e-35
LEAST = 110.0
BIAS = 128.0
SEND = ((2, 1, 0, 3), (0, 1, 3, 2), (0, 3, 2, 1), (1, 2, 3, 0))
ARRIVE = ((0, 1, 2, 3), (1, 0, 3, 2), (2, 3, 0, 1), (3, 2, 1, 0))
BACK = ((2, 3, 1, 0), (2, 3, 0, 1), (0, 1, 3, 2), (0, 1, 2, 3))
BF16 = jnp.bfloat16
F32 = jnp.float32
MESH = pl.DeviceIdType.MESH
SMEM = pl.BlockSpec(memory_space=pltpu.SMEM)
VMEM = pl.BlockSpec(memory_space=pltpu.VMEM)
TURN = 2.0 * np.pi
TURN_1 = float(np.float32(6.28125))
TURN_2 = float(np.float32(TURN - 6.28125))


def halves(values):
    high = values.astype(BF16)
    return (high, (values - high.astype(F32)).astype(BF16))


def cosine_table(cells):
    counter = np.arange(cells, dtype=np.int64)
    exact = np.cos(TURN / cells * (counter[:, None] * counter[None, :] % cells)) / cells
    high = exact.astype(np.float32).astype(jnp.bfloat16)
    low = (exact - high.astype(np.float64)).astype(np.float32).astype(jnp.bfloat16)
    return np.stack([high, low])


def dot(left, right):
    return jnp.dot(left, right, preferred_element_type=F32)


def dot3(left_high, left_low, right_high, right_low):
    return dot(left_high, right_high) + dot(left_high, right_low) + dot(left_low, right_high)


def cos_sin(phase):
    turns = jnp.floor(phase * (1.0 / TURN) + 0.5)
    rest = phase - turns * TURN_1 - turns * TURN_2
    return (jnp.cos(rest), jnp.sin(rest))


def ghost_scalars(reflect, curvature, position, wave, pair, case, ghost):
    start, turn = (pair[0, ghost], pair[1, ghost])
    coefficient = spread_scale * wave[case[ghost]] * (position[start] - position[turn])
    return (coefficient, curvature[turn], reflect[start] * reflect[turn])


def build_operator(cells, coefficient, power, table, spread, screened, both):
    counter = lax.broadcasted_iota(jnp.int32, (16, cells), 1)
    row = lax.broadcasted_iota(jnp.int32, (16, cells), 0)
    shifted = ((counter + cells // 2) % cells - cells // 2).astype(F32)
    cosine, sine = cos_sin(coefficient * (shifted * shifted / float(cells * cells)))
    transfer = jnp.where(row == 0, cosine, jnp.where(row == 1, -sine, 0.0))
    high, low = halves(transfer)
    kernel_rows = dot3(high, low, table[0], table[1])
    centred = (counter - cells // 2).astype(F32) / float(cells)
    screen_cos, screen_sin = cos_sin(power * (centred * centred))
    screen_cos, screen_sin = (screen_cos[0:1], screen_sin[0:1])
    step = 128
    for begin in range(0, cells, step):
        rows = pl.ds(begin, step)
        real, imag = (pltpu.roll(jnp.broadcast_to(kernel_rows[part:part + 1], (step, cells)), begin, 1, stride=1, stride_axis=0) for part in (0, 1))
        spread[0, rows, :], spread[1, rows, :] = halves(real)
        spread[2, rows, :], spread[3, rows, :] = halves(imag)
        screened[0, rows, :], screened[1, rows, :] = halves(real * screen_cos - imag * screen_sin)
        screened[2, rows, :], screened[3, rows, :] = halves(real * screen_sin + imag * screen_cos)
    wide = cells // 2

    @pl.loop(0, 2)
    def _(chunk):
        rows = pl.ds(pl.multiple_of(chunk * wide, wide), wide)
        left = [screened[k, rows, :] for k in range(4)]
        right = [spread[k] for k in range(4)]
        real = dot3(left[0], left[1], right[0], right[1]) - dot3(left[2], left[3], right[2], right[3])
        both[0, rows, :], both[1, rows, :] = halves(real)
        imag = dot3(left[0], left[1], right[2], right[3]) + dot3(left[2], left[3], right[0], right[1])
        both[2, rows, :], both[3, rows, :] = halves(imag)


def slab_first(real, imag, slab, both, middle, rows):
    tall = real.shape[0]
    stacked = jnp.concatenate([real, imag], axis=0)
    weights = [both[k, :, slab] for k in range(4)]
    by_real = dot(stacked, weights[0]) + dot(stacked, weights[1])
    by_imag = dot(stacked, weights[2]) + dot(stacked, weights[3])
    middle[0, rows, :], middle[1, rows, :] = halves(by_real[:tall] - by_imag[tall:])
    middle[2, rows, :], middle[3, rows, :] = halves(by_imag[:tall] + by_real[tall:])


def slab_second(both, middle, rows, depth):
    high = jnp.concatenate([both[0, rows, depth], both[2, rows, depth]], axis=0)
    low = jnp.concatenate([both[1, rows, depth], both[3, rows, depth]], axis=0)
    tall = high.shape[0] // 2
    by_real = dot3(high, low, middle[0, depth, :], middle[1, depth, :])
    by_imag = dot3(high, low, middle[2, depth, :], middle[3, depth, :])
    return (by_real[:tall] - by_imag[tall:], by_imag[:tall] + by_real[tall:])


def encode(values):
    peak = jnp.max(values, axis=1, keepdims=True)
    power = jnp.clip(jnp.floor(jnp.log2(jnp.maximum(peak, TINY))) + 1.0, -LEAST, LEAST)
    codes = jnp.minimum(values * jnp.exp2(15.0 - power) + 0.5, TOP).astype(jnp.int32)
    row = lax.broadcasted_iota(jnp.int32, values.shape, 1)
    bits = jnp.right_shift(jnp.broadcast_to((power + BIAS).astype(jnp.int32), values.shape), jnp.minimum(row, 8)) & 1
    return jnp.where(bits == 1, -1 - codes, codes).astype(jnp.int16)


def decode(codes):
    codes = codes.astype(jnp.int32)
    row = lax.broadcasted_iota(jnp.int32, codes.shape, 0)
    weight = jnp.left_shift(1, jnp.minimum(row, 8)).astype(F32)
    power = jnp.sum(jnp.where(codes < 0, weight, 0.0), axis=0, keepdims=True) - BIAS
    return jnp.where(codes < 0, -1 - codes, codes).astype(F32) * jnp.exp2(power - 15.0)


def scratch_of(cells, slab_cells):
    return [pltpu.VMEM((4, cells, cells), BF16), pltpu.VMEM((4, cells, cells), BF16), pltpu.VMEM((4, cells, cells), BF16), pltpu.VMEM((4, cells, slab_cells), BF16)]


def whole_kernel(cells, paths, row_count, field_hbm, table_hbm, *rest):
    small_hbm, (out, spread, screened, both, middle, field, table, *small), rest = (rest[:6], rest[6:19], rest[19:])
    outgoing, held, partial, bright, got, load_sem, send_sem, recv_sem, pass_send, pass_recv, out_send, out_recv, ready = rest
    reflect, curvature, position, wave, pair, case = small
    path, row = (lax.axis_index('path'), lax.axis_index('row'))
    chip, slab_id = (path // row_count, path % row_count)
    own = chip * row_count + row
    ghosts = case.shape[0]
    slab_cells = cells // row_count
    piece = cells // paths
    devices = paths * row_count
    mine = path * row_count + row
    is_home = slab_id == row
    group = paths // PARTS
    tall = cells // PARTS
    plane = path // group

    def order_of(other_path, other_row):
        if isinstance(other_path, int):
            hops = other_path // group + other_path % group // row_count + other_row
        else:
            inside = lax.div(lax.rem(other_path, group), row_count)
            hops = lax.div(other_path, group) + inside + other_row
        return hops * devices + other_path * row_count + other_row
    order = order_of(path, row)
    everyone = [(p, r) for p in range(paths) for r in range(row_count)]

    def plane_at(table, step):
        mine = table[-1][step]
        for other in range(PARTS - 1):
            mine = jnp.where(plane == other, table[other][step], mine)
        return mine
    loads = [pltpu.make_async_copy(source, target, load_sem.at[index]) for index, (source, target) in enumerate(zip((field_hbm, table_hbm, *small_hbm), (field, table, *small)))]
    for load in loads[:1] + loads[2:] + loads[1:2]:
        load.start()
    barrier = pltpu.get_barrier_semaphore()
    earlier = 0
    for other in everyone:
        is_later = order_of(*other) > order
        earlier += jnp.where(order_of(*other) < order, 1, 0)

        @pl.when(is_later)
        def _():
            pl.semaphore_signal(barrier, inc=1, device_id=other, device_id_type=MESH)

    @pl.when(earlier > 0)
    def _():
        pl.semaphore_wait(barrier, earlier)

    def say_ready(other_path, other_row):

        @pl.when(order_of(other_path, other_row) < order)
        def _():
            pl.semaphore_signal(ready.at[mine], inc=1, device_id=(other_path, other_row), device_id_type=MESH)
    for other_path in range(paths):
        say_ready(jnp.int32(other_path), slab_id)
    for turn in range(1, row_count):
        partner = chip * row_count + lax.rem(slab_id + turn, row_count)

        @pl.when(row != slab_id)
        def _():
            say_ready(partner, row)

    def field_target(ghost):
        return (lax.div(ghost, row_count) * row_count + row, lax.rem(ghost, row_count))

    def field_copy(ghost):
        return pltpu.make_async_remote_copy(src_ref=outgoing.at[ghost], dst_ref=held.at[row, path], send_sem=send_sem.at[ghost], recv_sem=recv_sem.at[path], device_id=field_target(ghost), device_id_type=MESH)

    def field_arrival(source):
        return pltpu.make_async_remote_copy(src_ref=outgoing.at[0], dst_ref=held.at[slab_id, source], send_sem=send_sem.at[0], recv_sem=recv_sem.at[source], device_id=(path, row), device_id_type=MESH)
    home_copy = pltpu.make_async_copy(outgoing.at[own], held.at[row, path], recv_sem.at[path])
    for load in loads[2:] + loads[:1]:
        load.wait()
    each = ghosts // PARTS
    turn_of = lax.rem(own, each)

    def send_plane(step):
        for turn in range(each):
            ghost = plane_at(SEND, step) * each + lax.rem(turn_of + turn, each)
            index = case[ghost] * SURF + pair[0, ghost]
            outgoing[ghost, 0] = field[0, index]
            outgoing[ghost, 1] = field[1, index]
            target_path, target_row = field_target(ghost)
            away = jnp.logical_or(ghost != own, jnp.logical_not(is_home))

            @pl.when(jnp.logical_and(away, order_of(target_path, target_row) > order))
            def _():
                pl.semaphore_wait(ready.at[target_path * row_count + target_row], 1)

            @pl.when(away)
            def _():
                field_copy(ghost).start()

            @pl.when(jnp.logical_not(away))
            def _():
                home_copy.start()

    def drain_plane(step, count):
        for turn in range(*count):
            ghost = plane_at(SEND, step) * each + lax.rem(turn_of + turn, each)

            @pl.when(jnp.logical_or(ghost != own, jnp.logical_not(is_home)))
            def _():
                field_copy(ghost).wait_send()
    for step in range(PARTS):
        send_plane(step)
    for turn in range(1, row_count):
        partner = chip * row_count + lax.rem(slab_id + turn, row_count)

        @pl.when(jnp.logical_and(lax.rem(partner, row_count) != row, order_of(partner, row) > order))
        def _():
            pl.semaphore_wait(ready.at[partner * row_count + row], 1)
    loads[1].wait()
    coefficient, power, gain = ghost_scalars(reflect, curvature, position, wave, pair, case, own)
    build_operator(cells, coefficient, power, table, spread, screened, both)

    def pass_copy(source, turn):
        return pltpu.make_async_remote_copy(src_ref=held.at[slab_id, source], dst_ref=held.at[slab_id, source], send_sem=pass_send.at[turn - 1, source], recv_sem=pass_recv.at[turn - 1, source], device_id=(chip * row_count + (slab_id + turn) % row_count, row), device_id_type=MESH)

    def pass_arrival(source, turn):
        return pltpu.make_async_remote_copy(src_ref=held.at[slab_id, source], dst_ref=held.at[(slab_id + row_count - turn) % row_count, source], send_sem=pass_send.at[turn - 1, source], recv_sem=pass_recv.at[turn - 1, source], device_id=(path, row), device_id_type=MESH)
    slab = pl.ds(pl.multiple_of(slab_id * slab_cells, slab_cells), slab_cells)

    def take_plane(step):
        for turn in range(group):
            source = plane_at(ARRIVE, step) * group + lax.rem(path + turn, group)

            @pl.when(jnp.logical_or(source != path, jnp.logical_not(is_home)))
            def _():
                field_arrival(source).wait_recv()

            @pl.when(jnp.logical_and(source == path, is_home))
            def _():
                home_copy.wait()
            for other in range(1, row_count):
                pass_copy(source, other).start()

    def first_plane(step):
        chunk = plane_at(ARRIVE, step)
        for turn in range(group):
            for other in range(1, row_count):
                pass_arrival(chunk * group + turn, other).wait_recv()

        def rows_of(part):
            return jnp.concatenate([held[side, pl.ds(chunk * group, group), part].reshape(tall, slab_cells) for side in range(row_count)], axis=1)
        rows = pl.ds(pl.multiple_of(chunk * tall, tall), tall)
        slab_first(rows_of(0), rows_of(1), slab, both, middle, rows)

    def half_at(index):
        return pl.ds(pl.multiple_of(index * (cells // 2), cells // 2), cells // 2)

    def half_second():

        @pl.loop(0, 2)
        def _(chunk):
            rows = half_at(chunk)
            real, imag = slab_second(both, middle, rows, half_at(plane // 2))
            partial[0, rows, :], partial[1, rows, :] = (real, imag)
    take_plane(0)
    take_plane(1)
    first_plane(0)
    first_plane(1)
    take_plane(2)
    half_second()
    first_plane(2)
    take_plane(3)
    first_plane(3)

    def bright_copies(target):
        return [pltpu.make_async_remote_copy(src_ref=source.at[target], dst_ref=arrived.at[own], send_sem=sent.at[target], recv_sem=received.at[own], device_id=(target, slab_id), device_id_type=MESH) for source, arrived, sent, received in ((bright, got, out_send, out_recv),)]

    def bright_arrivals(ghost):
        return [pltpu.make_async_remote_copy(src_ref=source.at[0], dst_ref=arrived.at[ghost], send_sem=sent.at[0], recv_sem=received.at[ghost], device_id=(path, row), device_id_type=MESH) for source, arrived, sent, received in ((bright, got, out_send, out_recv),)]
    home_bright = [pltpu.make_async_copy(bright.at[path], got.at[own], out_recv.at[own])]
    unit = gain * gain * (CASES / ghosts)
    for turned in range(PARTS):
        chunk = plane_at(BACK, turned)
        rows = pl.ds(pl.multiple_of(chunk * tall, tall), tall)
        real, imag = slab_second(both, middle, rows, half_at(1 - plane // 2))
        real, imag = (real + partial[0, rows, :], imag + partial[1, rows, :])
        intensity = (real * real + imag * imag).reshape(group, piece, slab_cells)
        bright[pl.ds(chunk * group, group)] = encode(intensity * unit)
        for step in range(group):
            target = chunk * group + lax.rem(path + step, group)

            @pl.when(jnp.logical_or(target != path, jnp.logical_not(is_home)))
            def _():
                for copy in bright_copies(target):
                    copy.start()

            @pl.when(jnp.logical_and(target == path, is_home))
            def _():
                for copy in home_bright:
                    copy.start()
    out[...] = jnp.zeros_like(out)
    for step in range(PARTS):
        drain_plane(step, (0, each))
    for source in range(paths):
        for turn in range(1, row_count):
            pass_copy(source, turn).wait_send()

    def drain_back(step):
        for turn in range(group):
            target = plane_at(BACK, step) * group + lax.rem(path + turn, group)

            @pl.when(jnp.logical_or(target != path, jnp.logical_not(is_home)))
            def _():
                for copy in bright_copies(target):
                    copy.wait_send()
    for step in range(ghosts):
        if step == ghosts - each:
            drain_back(0)
            drain_back(1)
        ghost = plane_at(ARRIVE, step // each) * each + lax.rem(turn_of + step, each)

        @pl.when(jnp.logical_or(ghost != own, jnp.logical_not(is_home)))
        def _():
            for copy in bright_arrivals(ghost):
                copy.wait_recv()

        @pl.when(jnp.logical_and(ghost == own, is_home))
        def _():
            for copy in home_bright:
                copy.wait()
        values = decode(got[ghost])
        for index in range(CASES):
            chosen = jnp.where(case[ghost] == index, 1.0, 0.0)
            out[index] += chosen * values
    for step in range(2, PARTS):
        drain_back(step)


def whole(cells, paths, row_count, main_field, table, *small):
    ghosts = small[-1].shape[0]
    piece, slab_cells = (cells // paths, cells // row_count)
    return pl.pallas_call(functools.partial(whole_kernel, cells, paths, row_count), out_shape=jax.ShapeDtypeStruct((CASES, piece, slab_cells), F32), in_specs=[pl.BlockSpec(memory_space=pltpu.HBM)] * 8, out_specs=VMEM, scratch_shapes=scratch_of(cells, slab_cells) + [pltpu.VMEM(main_field.shape, BF16), pltpu.VMEM((2, cells, cells), BF16), *[pltpu.SMEM(array.shape, array.dtype) for array in small], pltpu.VMEM((ghosts, 2, piece, slab_cells), BF16), pltpu.VMEM((row_count, paths, 2, piece, slab_cells), BF16), pltpu.VMEM((2, cells, slab_cells), F32), pltpu.VMEM((paths, piece, slab_cells), jnp.int16), pltpu.VMEM((ghosts, piece, slab_cells), jnp.int16), pltpu.SemaphoreType.DMA((8,)), pltpu.SemaphoreType.DMA((ghosts,)), pltpu.SemaphoreType.DMA((paths,)), pltpu.SemaphoreType.DMA((row_count - 1, paths)), pltpu.SemaphoreType.DMA((row_count - 1, paths)), pltpu.SemaphoreType.DMA((paths,)), pltpu.SemaphoreType.DMA((ghosts,)), pltpu.SemaphoreType.REGULAR((paths * row_count,))], compiler_params=pltpu.CompilerParams(collective_id=0, has_side_effects=True, vmem_limit_bytes=60 * 1024 * 1024))(main_field, table, *small)


def slab_kernel(cells, row_count, field, table, reflect, curvature, position, wave, pair, case, slot, out, spread, screened, both, middle):
    slab_cells = cells // row_count
    coefficient, power, gain = ghost_scalars(reflect, curvature, position, wave, pair, case, slot[0])
    build_operator(cells, coefficient, power, table, spread, screened, both)
    slab = pl.ds(pl.multiple_of(slot[1] * slab_cells, slab_cells), slab_cells)
    tall = cells // 2

    @pl.loop(0, 2)
    def _(chunk):
        rows = pl.ds(pl.multiple_of(chunk * tall, tall), tall)
        slab_first(field[0, rows, :], field[1, rows, :], slab, both, middle, rows)

    @pl.loop(0, 2)
    def _(chunk):
        rows = pl.ds(pl.multiple_of(chunk * tall, tall), tall)
        real, imag = slab_second(both, middle, rows, pl.ds(0, cells))
        out[rows, :] = gain * gain * (real * real + imag * imag)


def local(main_field, table, *small):
    paths = lax.axis_size('path')
    row_count = lax.axis_size('row')
    piece, slab_cells = main_field.shape[2:]
    cells = piece * paths
    pair, case = small[-2:]
    ghosts = case.shape[0]
    if piece % 16 == 0 and ghosts == paths and (paths % (PARTS * row_count) == 0) and (row_count > 1):
        return whole(cells, paths, row_count, main_field, table, *small)
    per_device = ghosts // paths
    fields = jnp.arange(main_field.shape[1], dtype=jnp.int32)
    wanted = (fields[None, :] == (case * SURF + pair[0])[:, None]).astype(BF16)
    picked = jnp.einsum('gf,cfrv->cgrv', wanted, main_field, preferred_element_type=F32).astype(BF16)
    picked = picked.reshape(2, paths, per_device, piece, slab_cells)
    arrived = lax.all_to_all(picked, 'path', split_axis=1, concat_axis=3, tiled=True)
    fields = lax.all_gather(arrived.reshape(2, per_device, cells, slab_cells), 'row', axis=3, tiled=True)
    bright = []
    for index in range(per_device):
        slot = jnp.stack([lax.axis_index('path') * per_device + index, lax.axis_index('row')])
        bright.append(pl.pallas_call(functools.partial(slab_kernel, cells, row_count), out_shape=jax.ShapeDtypeStruct((cells, slab_cells), F32), in_specs=[VMEM, VMEM] + [SMEM] * 7, out_specs=VMEM, scratch_shapes=scratch_of(cells, slab_cells), compiler_params=pltpu.CompilerParams(vmem_limit_bytes=48 * 1024 * 1024))(fields[:, index], table, *small, slot))
    got = lax.all_to_all(jnp.stack(bright), 'path', split_axis=1, concat_axis=0, tiled=True)
    got = got.reshape(paths, per_device, piece, slab_cells).reshape(ghosts, piece, slab_cells)
    chosen = (case[:, None] == jnp.arange(CASES, dtype=jnp.int32)).astype(F32)
    total = jnp.sum(chosen[:, :, None, None] * got[:, None], 0)
    return total * (CASES / ghosts)


def solution(mesh):
    in_specs = (P(None, None, 'path', 'row'), P(), P(), P(), P(), P(), P())
    out_specs = P(None, 'path', 'row')

    def run(main_field, reflect, curvature, position, wave, pair, case):
        small = (reflect, curvature, position, wave, pair.T, case)
        table = cosine_table(main_field.shape[2] * mesh.shape['path'])
        return local(main_field, jnp.asarray(table), *small)
    return jax.shard_map(run, mesh=mesh, in_specs=in_specs, out_specs=out_specs, check_vma=False)
```

```python
import functools
import jax
import jax.numpy as jnp
import numpy as np
from jax import lax
from jax.experimental import pallas as pl
from jax.experimental.pallas import tpu as pltpu
from jax.sharding import PartitionSpec as P
CASES = 4
SURF = 9
spread_scale = 2000.0
PARTS = 4
TOP = 32767.0
TINY = 1e-35
LEAST = 110.0
BIAS = 128.0
SEND = ((2, 1, 0, 3), (0, 1, 3, 2), (0, 3, 2, 1), (1, 2, 3, 0))
ARRIVE = ((0, 1, 2, 3), (1, 0, 3, 2), (2, 3, 0, 1), (3, 2, 1, 0))
BACK = ((2, 3, 0, 1), (0, 2, 3, 1), (0, 1, 3, 2), (0, 1, 2, 3))
BF16 = jnp.bfloat16
F32 = jnp.float32
MESH = pl.DeviceIdType.MESH
SMEM = pl.BlockSpec(memory_space=pltpu.SMEM)
VMEM = pl.BlockSpec(memory_space=pltpu.VMEM)
TURN = 2.0 * np.pi
TURN_1 = float(np.float32(6.28125))
TURN_2 = float(np.float32(TURN - 6.28125))


def halves(values):
    high = values.astype(BF16)
    return (high, (values - high.astype(F32)).astype(BF16))


def cosine_table(cells):
    counter = np.arange(cells, dtype=np.int64)
    exact = np.cos(TURN / cells * (counter[:, None] * counter[None, :] % cells)) / cells
    high = exact.astype(np.float32).astype(jnp.bfloat16)
    low = (exact - high.astype(np.float64)).astype(np.float32).astype(jnp.bfloat16)
    return np.stack([high, low])


def dot(left, right):
    return jnp.dot(left, right, preferred_element_type=F32)


def dot3(left_high, left_low, right_high, right_low):
    return dot(left_high, right_high) + dot(left_high, right_low) + dot(left_low, right_high)


def cos_sin(phase):
    turns = jnp.floor(phase * (1.0 / TURN) + 0.5)
    rest = phase - turns * TURN_1 - turns * TURN_2
    return (jnp.cos(rest), jnp.sin(rest))


def ghost_scalars(reflect, curvature, position, wave, pair, case, ghost):
    start, turn = (pair[0, ghost], pair[1, ghost])
    coefficient = spread_scale * wave[case[ghost]] * (position[start] - position[turn])
    return (coefficient, curvature[turn], reflect[start] * reflect[turn])


def build_operator(cells, coefficient, power, table, spread, screened, both):
    counter = lax.broadcasted_iota(jnp.int32, (16, cells), 1)
    row = lax.broadcasted_iota(jnp.int32, (16, cells), 0)
    shifted = ((counter + cells // 2) % cells - cells // 2).astype(F32)
    cosine, sine = cos_sin(coefficient * (shifted * shifted / float(cells * cells)))
    transfer = jnp.where(row == 0, cosine, jnp.where(row == 1, -sine, 0.0))
    high, low = halves(transfer)
    kernel_rows = dot3(high, low, table[0], table[1])
    centred = (counter - cells // 2).astype(F32) / float(cells)
    screen_cos, screen_sin = cos_sin(power * (centred * centred))
    screen_cos, screen_sin = (screen_cos[0:1], screen_sin[0:1])
    step = 128
    for begin in range(0, cells, step):
        rows = pl.ds(begin, step)
        real, imag = (pltpu.roll(jnp.broadcast_to(kernel_rows[part:part + 1], (step, cells)), begin, 1, stride=1, stride_axis=0) for part in (0, 1))
        spread[0, rows, :], spread[1, rows, :] = halves(real)
        spread[2, rows, :], spread[3, rows, :] = halves(imag)
        screened[0, rows, :], screened[1, rows, :] = halves(real * screen_cos - imag * screen_sin)
        screened[2, rows, :], screened[3, rows, :] = halves(real * screen_sin + imag * screen_cos)
    wide = cells // 2

    @pl.loop(0, 2)
    def _(chunk):
        rows = pl.ds(pl.multiple_of(chunk * wide, wide), wide)
        left = [screened[k, rows, :] for k in range(4)]
        right = [spread[k] for k in range(4)]
        real = dot3(left[0], left[1], right[0], right[1]) - dot3(left[2], left[3], right[2], right[3])
        both[0, rows, :], both[1, rows, :] = halves(real)
        imag = dot3(left[0], left[1], right[2], right[3]) + dot3(left[2], left[3], right[0], right[1])
        both[2, rows, :], both[3, rows, :] = halves(imag)


def slab_first(real, imag, slab, both, middle, rows):
    tall = real.shape[0]
    stacked = jnp.concatenate([real, imag], axis=0)
    weights = [both[k, :, slab] for k in range(4)]
    by_real = dot(stacked, weights[0]) + dot(stacked, weights[1])
    by_imag = dot(stacked, weights[2]) + dot(stacked, weights[3])
    middle[0, rows, :], middle[1, rows, :] = halves(by_real[:tall] - by_imag[tall:])
    middle[2, rows, :], middle[3, rows, :] = halves(by_imag[:tall] + by_real[tall:])


def slab_second(both, middle, rows, depth):
    high = jnp.concatenate([both[0, rows, depth], both[2, rows, depth]], axis=0)
    low = jnp.concatenate([both[1, rows, depth], both[3, rows, depth]], axis=0)
    tall = high.shape[0] // 2
    by_real = dot3(high, low, middle[0, depth, :], middle[1, depth, :])
    by_imag = dot3(high, low, middle[2, depth, :], middle[3, depth, :])
    return (by_real[:tall] - by_imag[tall:], by_imag[:tall] + by_real[tall:])


def encode(values):
    peak = jnp.max(values, axis=1, keepdims=True)
    power = jnp.clip(jnp.floor(jnp.log2(jnp.maximum(peak, TINY))) + 1.0, -LEAST, LEAST)
    codes = jnp.minimum(values * jnp.exp2(15.0 - power) + 0.5, TOP).astype(jnp.int32)
    row = lax.broadcasted_iota(jnp.int32, values.shape, 1)
    bits = jnp.right_shift(jnp.broadcast_to((power + BIAS).astype(jnp.int32), values.shape), jnp.minimum(row, 8)) & 1
    return jnp.where(bits == 1, -1 - codes, codes).astype(jnp.int16)


def decode(codes):
    codes = codes.astype(jnp.int32)
    row = lax.broadcasted_iota(jnp.int32, codes.shape, 0)
    weight = jnp.left_shift(1, jnp.minimum(row, 8)).astype(F32)
    power = jnp.sum(jnp.where(codes < 0, weight, 0.0), axis=0, keepdims=True) - BIAS
    return jnp.where(codes < 0, -1 - codes, codes).astype(F32) * jnp.exp2(power - 15.0)


def scratch_of(cells, slab_cells):
    return [pltpu.VMEM((4, cells, cells), BF16), pltpu.VMEM((4, cells, cells), BF16), pltpu.VMEM((4, cells, cells), BF16), pltpu.VMEM((4, cells, slab_cells), BF16)]


def whole_kernel(cells, paths, row_count, field_hbm, table_hbm, *rest):
    small_hbm, (out, spread, screened, both, middle, field, table, *small), rest = (rest[:6], rest[6:19], rest[19:])
    outgoing, held, partial, bright, got, load_sem, send_sem, recv_sem, pass_send, pass_recv, out_send, out_recv, ready = rest
    reflect, curvature, position, wave, pair, case = small
    path, row = (lax.axis_index('path'), lax.axis_index('row'))
    chip, slab_id = (path // row_count, path % row_count)
    own = chip * row_count + row
    ghosts = case.shape[0]
    slab_cells = cells // row_count
    piece = cells // paths
    devices = paths * row_count
    mine = path * row_count + row
    is_home = slab_id == row
    group = paths // PARTS
    tall = cells // PARTS
    plane = path // group

    def order_of(other_path, other_row):
        if isinstance(other_path, int):
            hops = other_path // group + other_path % group // row_count + other_row
        else:
            inside = lax.div(lax.rem(other_path, group), row_count)
            hops = lax.div(other_path, group) + inside + other_row
        return hops * devices + other_path * row_count + other_row
    order = order_of(path, row)
    everyone = [(p, r) for p in range(paths) for r in range(row_count)]

    def plane_at(table, step):
        mine = table[-1][step]
        for other in range(PARTS - 1):
            mine = jnp.where(plane == other, table[other][step], mine)
        return mine
    loads = [pltpu.make_async_copy(source, target, load_sem.at[index]) for index, (source, target) in enumerate(zip((field_hbm, table_hbm, *small_hbm), (field, table, *small)))]
    for load in loads[:1] + loads[2:] + loads[1:2]:
        load.start()
    barrier = pltpu.get_barrier_semaphore()
    earlier = 0
    for other in everyone:
        is_later = order_of(*other) > order
        earlier += jnp.where(order_of(*other) < order, 1, 0)

        @pl.when(is_later)
        def _():
            pl.semaphore_signal(barrier, inc=1, device_id=other, device_id_type=MESH)

    @pl.when(earlier > 0)
    def _():
        pl.semaphore_wait(barrier, earlier)

    def say_ready(other_path, other_row):

        @pl.when(order_of(other_path, other_row) < order)
        def _():
            pl.semaphore_signal(ready.at[mine], inc=1, device_id=(other_path, other_row), device_id_type=MESH)
    for other_path in range(paths):
        say_ready(jnp.int32(other_path), slab_id)
    for turn in range(1, row_count):
        partner = chip * row_count + lax.rem(slab_id + turn, row_count)

        @pl.when(row != slab_id)
        def _():
            say_ready(partner, row)

    def field_target(ghost):
        return (lax.div(ghost, row_count) * row_count + row, lax.rem(ghost, row_count))

    def field_copy(ghost):
        return pltpu.make_async_remote_copy(src_ref=outgoing.at[ghost], dst_ref=held.at[row, path], send_sem=send_sem.at[ghost], recv_sem=recv_sem.at[path], device_id=field_target(ghost), device_id_type=MESH)

    def field_arrival(source):
        return pltpu.make_async_remote_copy(src_ref=outgoing.at[0], dst_ref=held.at[slab_id, source], send_sem=send_sem.at[0], recv_sem=recv_sem.at[source], device_id=(path, row), device_id_type=MESH)
    home_copy = pltpu.make_async_copy(outgoing.at[own], held.at[row, path], recv_sem.at[path])
    for load in loads[2:] + loads[:1]:
        load.wait()
    each = ghosts // PARTS
    turn_of = lax.rem(own, each)

    def send_plane(step):
        for turn in range(each):
            ghost = plane_at(SEND, step) * each + lax.rem(turn_of + turn, each)
            index = case[ghost] * SURF + pair[0, ghost]
            outgoing[ghost, 0] = field[0, index]
            outgoing[ghost, 1] = field[1, index]
            target_path, target_row = field_target(ghost)
            away = jnp.logical_or(ghost != own, jnp.logical_not(is_home))

            @pl.when(jnp.logical_and(away, order_of(target_path, target_row) > order))
            def _():
                pl.semaphore_wait(ready.at[target_path * row_count + target_row], 1)

            @pl.when(away)
            def _():
                field_copy(ghost).start()

            @pl.when(jnp.logical_not(away))
            def _():
                home_copy.start()

    def drain_plane(step, count):
        for turn in range(*count):
            ghost = plane_at(SEND, step) * each + lax.rem(turn_of + turn, each)

            @pl.when(jnp.logical_or(ghost != own, jnp.logical_not(is_home)))
            def _():
                field_copy(ghost).wait_send()
    for step in range(PARTS):
        send_plane(step)
    for turn in range(1, row_count):
        partner = chip * row_count + lax.rem(slab_id + turn, row_count)

        @pl.when(jnp.logical_and(lax.rem(partner, row_count) != row, order_of(partner, row) > order))
        def _():
            pl.semaphore_wait(ready.at[partner * row_count + row], 1)
    loads[1].wait()
    coefficient, power, gain = ghost_scalars(reflect, curvature, position, wave, pair, case, own)
    build_operator(cells, coefficient, power, table, spread, screened, both)

    def pass_copy(source, turn, count=1):
        return pltpu.make_async_remote_copy(src_ref=held.at[slab_id, pl.ds(source, count)], dst_ref=held.at[slab_id, pl.ds(source, count)], send_sem=pass_send.at[turn - 1, source], recv_sem=pass_recv.at[turn - 1, source], device_id=(chip * row_count + (slab_id + turn) % row_count, row), device_id_type=MESH)

    def pass_arrival(source, turn, count=1):
        return pltpu.make_async_remote_copy(src_ref=held.at[slab_id, pl.ds(source, count)], dst_ref=held.at[(slab_id + row_count - turn) % row_count, pl.ds(source, count)], send_sem=pass_send.at[turn - 1, source], recv_sem=pass_recv.at[turn - 1, source], device_id=(path, row), device_id_type=MESH)
    slab = pl.ds(pl.multiple_of(slab_id * slab_cells, slab_cells), slab_cells)

    def take_plane(step):
        for turn in range(group):
            source = plane_at(ARRIVE, step) * group + lax.rem(path + turn, group)

            @pl.when(jnp.logical_or(source != path, jnp.logical_not(is_home)))
            def _():
                field_arrival(source).wait_recv()

            @pl.when(jnp.logical_and(source == path, is_home))
            def _():
                home_copy.wait()
            if step == PARTS - 1:
                for other in range(1, row_count):
                    pass_copy(source, other).start()
        if step < PARTS - 1:
            for other in range(1, row_count):
                pass_copy(plane_at(ARRIVE, step) * group, other, group).start()

    def first_plane(step):
        chunk = plane_at(ARRIVE, step)
        count = group if step < PARTS - 1 else 1
        for turn in range(0, group, count):
            for other in range(1, row_count):
                pass_arrival(chunk * group + turn, other, count).wait_recv()

        def rows_of(part):
            return jnp.concatenate([held[side, pl.ds(chunk * group, group), part].reshape(tall, slab_cells) for side in range(row_count)], axis=1)
        rows = pl.ds(pl.multiple_of(chunk * tall, tall), tall)
        slab_first(rows_of(0), rows_of(1), slab, both, middle, rows)

    def half_at(index):
        return pl.ds(pl.multiple_of(index * (cells // 2), cells // 2), cells // 2)

    def half_second():

        @pl.loop(0, 2)
        def _(chunk):
            rows = half_at(chunk)
            real, imag = slab_second(both, middle, rows, half_at(plane // 2))
            partial[0, rows, :], partial[1, rows, :] = (real, imag)
    take_plane(0)
    take_plane(1)
    first_plane(0)
    first_plane(1)
    take_plane(2)
    half_second()
    first_plane(2)
    take_plane(3)
    first_plane(3)

    def bright_copies(target):
        return [pltpu.make_async_remote_copy(src_ref=source.at[target], dst_ref=arrived.at[own], send_sem=sent.at[target], recv_sem=received.at[own], device_id=(target, slab_id), device_id_type=MESH) for source, arrived, sent, received in ((bright, got, out_send, out_recv),)]

    def bright_arrivals(ghost):
        return [pltpu.make_async_remote_copy(src_ref=source.at[0], dst_ref=arrived.at[ghost], send_sem=sent.at[0], recv_sem=received.at[ghost], device_id=(path, row), device_id_type=MESH) for source, arrived, sent, received in ((bright, got, out_send, out_recv),)]
    home_bright = [pltpu.make_async_copy(bright.at[path], got.at[own], out_recv.at[own])]
    unit = gain * gain * (CASES / ghosts)
    for turned in range(PARTS):
        chunk = plane_at(BACK, turned)
        rows = pl.ds(pl.multiple_of(chunk * tall, tall), tall)
        real, imag = slab_second(both, middle, rows, half_at(1 - plane // 2))
        real, imag = (real + partial[0, rows, :], imag + partial[1, rows, :])
        intensity = (real * real + imag * imag).reshape(group, piece, slab_cells)
        bright[pl.ds(chunk * group, group)] = encode(intensity * unit)
        for step in range(group):
            target = chunk * group + lax.rem(path + step, group)

            @pl.when(jnp.logical_or(target != path, jnp.logical_not(is_home)))
            def _():
                for copy in bright_copies(target):
                    copy.start()

            @pl.when(jnp.logical_and(target == path, is_home))
            def _():
                for copy in home_bright:
                    copy.start()
    out[...] = jnp.zeros_like(out)
    for step in range(PARTS):
        drain_plane(step, (0, each))
    for step in range(PARTS):
        count = group if step < PARTS - 1 else 1
        for source in range(0, group, count):
            for turn in range(1, row_count):
                pass_copy(plane_at(ARRIVE, step) * group + source, turn, count).wait_send()

    def drain_back(step):
        for turn in range(group):
            target = plane_at(BACK, step) * group + lax.rem(path + turn, group)

            @pl.when(jnp.logical_or(target != path, jnp.logical_not(is_home)))
            def _():
                for copy in bright_copies(target):
                    copy.wait_send()
    for step in range(ghosts):
        if step == ghosts - each:
            drain_back(0)
            drain_back(1)
        ghost = plane_at(ARRIVE, step // each) * each + lax.rem(turn_of + step, each)

        @pl.when(jnp.logical_or(ghost != own, jnp.logical_not(is_home)))
        def _():
            for copy in bright_arrivals(ghost):
                copy.wait_recv()

        @pl.when(jnp.logical_and(ghost == own, is_home))
        def _():
            for copy in home_bright:
                copy.wait()
        values = decode(got[ghost])
        for index in range(CASES):
            chosen = jnp.where(case[ghost] == index, 1.0, 0.0)
            out[index] += chosen * values
    for step in range(2, PARTS):
        drain_back(step)


def whole(cells, paths, row_count, main_field, table, *small):
    ghosts = small[-1].shape[0]
    piece, slab_cells = (cells // paths, cells // row_count)
    return pl.pallas_call(functools.partial(whole_kernel, cells, paths, row_count), out_shape=jax.ShapeDtypeStruct((CASES, piece, slab_cells), F32), in_specs=[pl.BlockSpec(memory_space=pltpu.HBM)] * 8, out_specs=VMEM, scratch_shapes=scratch_of(cells, slab_cells) + [pltpu.VMEM(main_field.shape, BF16), pltpu.VMEM((2, cells, cells), BF16), *[pltpu.SMEM(array.shape, array.dtype) for array in small], pltpu.VMEM((ghosts, 2, piece, slab_cells), BF16), pltpu.VMEM((row_count, paths, 2, piece, slab_cells), BF16), pltpu.VMEM((2, cells, slab_cells), F32), pltpu.VMEM((paths, piece, slab_cells), jnp.int16), pltpu.VMEM((ghosts, piece, slab_cells), jnp.int16), pltpu.SemaphoreType.DMA((8,)), pltpu.SemaphoreType.DMA((ghosts,)), pltpu.SemaphoreType.DMA((paths,)), pltpu.SemaphoreType.DMA((row_count - 1, paths)), pltpu.SemaphoreType.DMA((row_count - 1, paths)), pltpu.SemaphoreType.DMA((paths,)), pltpu.SemaphoreType.DMA((ghosts,)), pltpu.SemaphoreType.REGULAR((paths * row_count,))], compiler_params=pltpu.CompilerParams(collective_id=0, has_side_effects=True, vmem_limit_bytes=60 * 1024 * 1024))(main_field, table, *small)


def slab_kernel(cells, row_count, field, table, reflect, curvature, position, wave, pair, case, slot, out, spread, screened, both, middle):
    slab_cells = cells // row_count
    coefficient, power, gain = ghost_scalars(reflect, curvature, position, wave, pair, case, slot[0])
    build_operator(cells, coefficient, power, table, spread, screened, both)
    slab = pl.ds(pl.multiple_of(slot[1] * slab_cells, slab_cells), slab_cells)
    tall = cells // 2

    @pl.loop(0, 2)
    def _(chunk):
        rows = pl.ds(pl.multiple_of(chunk * tall, tall), tall)
        slab_first(field[0, rows, :], field[1, rows, :], slab, both, middle, rows)

    @pl.loop(0, 2)
    def _(chunk):
        rows = pl.ds(pl.multiple_of(chunk * tall, tall), tall)
        real, imag = slab_second(both, middle, rows, pl.ds(0, cells))
        out[rows, :] = gain * gain * (real * real + imag * imag)


def local(main_field, table, *small):
    paths = lax.axis_size('path')
    row_count = lax.axis_size('row')
    piece, slab_cells = main_field.shape[2:]
    cells = piece * paths
    pair, case = small[-2:]
    ghosts = case.shape[0]
    if piece % 16 == 0 and ghosts == paths and (paths % (PARTS * row_count) == 0) and (row_count > 1):
        return whole(cells, paths, row_count, main_field, table, *small)
    per_device = ghosts // paths
    fields = jnp.arange(main_field.shape[1], dtype=jnp.int32)
    wanted = (fields[None, :] == (case * SURF + pair[0])[:, None]).astype(BF16)
    picked = jnp.einsum('gf,cfrv->cgrv', wanted, main_field, preferred_element_type=F32).astype(BF16)
    picked = picked.reshape(2, paths, per_device, piece, slab_cells)
    arrived = lax.all_to_all(picked, 'path', split_axis=1, concat_axis=3, tiled=True)
    fields = lax.all_gather(arrived.reshape(2, per_device, cells, slab_cells), 'row', axis=3, tiled=True)
    bright = []
    for index in range(per_device):
        slot = jnp.stack([lax.axis_index('path') * per_device + index, lax.axis_index('row')])
        bright.append(pl.pallas_call(functools.partial(slab_kernel, cells, row_count), out_shape=jax.ShapeDtypeStruct((cells, slab_cells), F32), in_specs=[VMEM, VMEM] + [SMEM] * 7, out_specs=VMEM, scratch_shapes=scratch_of(cells, slab_cells), compiler_params=pltpu.CompilerParams(vmem_limit_bytes=48 * 1024 * 1024))(fields[:, index], table, *small, slot))
    got = lax.all_to_all(jnp.stack(bright), 'path', split_axis=1, concat_axis=0, tiled=True)
    got = got.reshape(paths, per_device, piece, slab_cells).reshape(ghosts, piece, slab_cells)
    chosen = (case[:, None] == jnp.arange(CASES, dtype=jnp.int32)).astype(F32)
    total = jnp.sum(chosen[:, :, None, None] * got[:, None], 0)
    return total * (CASES / ghosts)


def solution(mesh):
    in_specs = (P(None, None, 'path', 'row'), P(), P(), P(), P(), P(), P())
    out_specs = P(None, 'path', 'row')

    def run(main_field, reflect, curvature, position, wave, pair, case):
        small = (reflect, curvature, position, wave, pair.T, case)
        table = cosine_table(main_field.shape[2] * mesh.shape['path'])
        return local(main_field, jnp.asarray(table), *small)
    return jax.shard_map(run, mesh=mesh, in_specs=in_specs, out_specs=out_specs, check_vma=False)
```

```python
import functools
import jax
import jax.numpy as jnp
import numpy as np
from jax import lax
from jax.experimental import pallas as pl
from jax.experimental.pallas import tpu as pltpu
from jax.sharding import PartitionSpec as P
CASES = 4
SURF = 9
spread_scale = 2000.0
PARTS = 4
TOP = 32767.0
TINY = 1e-35
LEAST = 110.0
BIAS = 128.0
SEND = ((2, 1, 0, 3), (0, 1, 3, 2), (0, 3, 2, 1), (1, 2, 3, 0))
ARRIVE = ((0, 1, 2, 3), (1, 0, 3, 2), (2, 3, 0, 1), (3, 2, 1, 0))
BACK = ((2, 3, 1, 0), (2, 3, 0, 1), (0, 1, 3, 2), (0, 1, 2, 3))
BF16 = jnp.bfloat16
F32 = jnp.float32
MESH = pl.DeviceIdType.MESH
SMEM = pl.BlockSpec(memory_space=pltpu.SMEM)
VMEM = pl.BlockSpec(memory_space=pltpu.VMEM)
TURN = 2.0 * np.pi
TURN_1 = float(np.float32(6.28125))
TURN_2 = float(np.float32(TURN - 6.28125))


def halves(values):
    high = values.astype(BF16)
    return (high, (values - high.astype(F32)).astype(BF16))


def cosine_table(cells):
    counter = np.arange(cells, dtype=np.int64)
    exact = np.cos(TURN / cells * (counter[:, None] * counter[None, :] % cells)) / cells
    high = exact.astype(np.float32).astype(jnp.bfloat16)
    low = (exact - high.astype(np.float64)).astype(np.float32).astype(jnp.bfloat16)
    return np.stack([high, low])


def dot(left, right):
    return jnp.dot(left, right, preferred_element_type=F32)


def dot3(left_high, left_low, right_high, right_low):
    return dot(left_high, right_high) + dot(left_high, right_low) + dot(left_low, right_high)


def cos_sin(phase):
    turns = jnp.floor(phase * (1.0 / TURN) + 0.5)
    rest = phase - turns * TURN_1 - turns * TURN_2
    return (jnp.cos(rest), jnp.sin(rest))


def ghost_scalars(reflect, curvature, position, wave, pair, case, ghost):
    start, turn = (pair[0, ghost], pair[1, ghost])
    coefficient = spread_scale * wave[case[ghost]] * (position[start] - position[turn])
    return (coefficient, curvature[turn], reflect[start] * reflect[turn])


def build_operator(cells, coefficient, power, table, spread, screened, both):
    counter = lax.broadcasted_iota(jnp.int32, (16, cells), 1)
    row = lax.broadcasted_iota(jnp.int32, (16, cells), 0)
    shifted = ((counter + cells // 2) % cells - cells // 2).astype(F32)
    cosine, sine = cos_sin(coefficient * (shifted * shifted / float(cells * cells)))
    transfer = jnp.where(row == 0, cosine, jnp.where(row == 1, -sine, 0.0))
    high, low = halves(transfer)
    kernel_rows = dot3(high, low, table[0], table[1])
    centred = (counter - cells // 2).astype(F32) / float(cells)
    screen_cos, screen_sin = cos_sin(power * (centred * centred))
    screen_cos, screen_sin = (screen_cos[0:1], screen_sin[0:1])
    step = 128
    for begin in range(0, cells, step):
        rows = pl.ds(begin, step)
        real, imag = (pltpu.roll(jnp.broadcast_to(kernel_rows[part:part + 1], (step, cells)), begin, 1, stride=1, stride_axis=0) for part in (0, 1))
        spread[0, rows, :], spread[1, rows, :] = halves(real)
        spread[2, rows, :], spread[3, rows, :] = halves(imag)
        screened[0, rows, :], screened[1, rows, :] = halves(real * screen_cos - imag * screen_sin)
        screened[2, rows, :], screened[3, rows, :] = halves(real * screen_sin + imag * screen_cos)
    wide = cells // 2

    @pl.loop(0, 2)
    def _(chunk):
        rows = pl.ds(pl.multiple_of(chunk * wide, wide), wide)
        left = [screened[k, rows, :] for k in range(4)]
        right = [spread[k] for k in range(4)]
        real = dot3(left[0], left[1], right[0], right[1]) - dot3(left[2], left[3], right[2], right[3])
        both[0, rows, :], both[1, rows, :] = halves(real)
        imag = dot3(left[0], left[1], right[2], right[3]) + dot3(left[2], left[3], right[0], right[1])
        both[2, rows, :], both[3, rows, :] = halves(imag)


def slab_first(real, imag, slab, both, middle, rows):
    tall = real.shape[0]
    stacked = jnp.concatenate([real, imag], axis=0)
    weights = [both[k, :, slab] for k in range(4)]
    by_real = dot(stacked, weights[0]) + dot(stacked, weights[1])
    by_imag = dot(stacked, weights[2]) + dot(stacked, weights[3])
    middle[0, rows, :], middle[1, rows, :] = halves(by_real[:tall] - by_imag[tall:])
    middle[2, rows, :], middle[3, rows, :] = halves(by_imag[:tall] + by_real[tall:])


def slab_second(both, middle, rows, depth):
    high = jnp.concatenate([both[0, rows, depth], both[2, rows, depth]], axis=0)
    low = jnp.concatenate([both[1, rows, depth], both[3, rows, depth]], axis=0)
    tall = high.shape[0] // 2
    by_real = dot3(high, low, middle[0, depth, :], middle[1, depth, :])
    by_imag = dot3(high, low, middle[2, depth, :], middle[3, depth, :])
    return (by_real[:tall] - by_imag[tall:], by_imag[:tall] + by_real[tall:])


def encode(values):
    peak = jnp.max(values, axis=1, keepdims=True)
    power = jnp.clip(jnp.floor(jnp.log2(jnp.maximum(peak, TINY))) + 1.0, -LEAST, LEAST)
    codes = jnp.minimum(values * jnp.exp2(15.0 - power) + 0.5, TOP).astype(jnp.int32)
    row = lax.broadcasted_iota(jnp.int32, values.shape, 1)
    bits = jnp.right_shift(jnp.broadcast_to((power + BIAS).astype(jnp.int32), values.shape), jnp.minimum(row, 8)) & 1
    return jnp.where(bits == 1, -1 - codes, codes).astype(jnp.int16)


def decode(codes):
    codes = codes.astype(jnp.int32)
    row = lax.broadcasted_iota(jnp.int32, codes.shape, 0)
    weight = jnp.left_shift(1, jnp.minimum(row, 8)).astype(F32)
    power = jnp.sum(jnp.where(codes < 0, weight, 0.0), axis=0, keepdims=True) - BIAS
    return jnp.where(codes < 0, -1 - codes, codes).astype(F32) * jnp.exp2(power - 15.0)


def scratch_of(cells, slab_cells):
    return [pltpu.VMEM((4, cells, cells), BF16), pltpu.VMEM((4, cells, cells), BF16), pltpu.VMEM((4, cells, cells), BF16), pltpu.VMEM((4, cells, slab_cells), BF16)]


def whole_kernel(cells, paths, row_count, field_hbm, table_hbm, *rest):
    small_hbm, (out, spread, screened, both, middle, field, table, *small), rest = (rest[:6], rest[6:19], rest[19:])
    outgoing, held, partial, bright, got, load_sem, send_sem, recv_sem, pass_send, pass_recv, out_send, out_recv, ready = rest
    reflect, curvature, position, wave, pair, case = small
    path, row = (lax.axis_index('path'), lax.axis_index('row'))
    chip, slab_id = (path // row_count, path % row_count)
    own = chip * row_count + row
    ghosts = case.shape[0]
    slab_cells = cells // row_count
    piece = cells // paths
    devices = paths * row_count
    mine = path * row_count + row
    is_home = slab_id == row
    group = paths // PARTS
    tall = cells // PARTS
    plane = path // group

    def order_of(other_path, other_row):
        if isinstance(other_path, int):
            hops = other_path // group + other_path % group // row_count + other_row
        else:
            inside = lax.div(lax.rem(other_path, group), row_count)
            hops = lax.div(other_path, group) + inside + other_row
        return hops * devices + other_path * row_count + other_row
    order = order_of(path, row)
    everyone = [(p, r) for p in range(paths) for r in range(row_count)]

    def plane_at(table, step):
        mine = table[-1][step]
        for other in range(PARTS - 1):
            mine = jnp.where(plane == other, table[other][step], mine)
        return mine
    loads = [pltpu.make_async_copy(source, target, load_sem.at[index]) for index, (source, target) in enumerate(zip((field_hbm, table_hbm, *small_hbm), (field, table, *small)))]
    for load in loads[:1] + loads[2:] + loads[1:2]:
        load.start()
    barrier = pltpu.get_barrier_semaphore()
    earlier = 0
    for other in everyone:
        is_later = order_of(*other) > order
        earlier += jnp.where(order_of(*other) < order, 1, 0)

        @pl.when(is_later)
        def _():
            pl.semaphore_signal(barrier, inc=1, device_id=other, device_id_type=MESH)

    @pl.when(earlier > 0)
    def _():
        pl.semaphore_wait(barrier, earlier)

    def say_ready(other_path, other_row):

        @pl.when(order_of(other_path, other_row) < order)
        def _():
            pl.semaphore_signal(ready.at[mine], inc=1, device_id=(other_path, other_row), device_id_type=MESH)
    for other_path in range(paths):
        say_ready(jnp.int32(other_path), slab_id)
    for turn in range(1, row_count):
        partner = chip * row_count + lax.rem(slab_id + turn, row_count)

        @pl.when(row != slab_id)
        def _():
            say_ready(partner, row)

    def field_target(ghost):
        return (lax.div(ghost, row_count) * row_count + row, lax.rem(ghost, row_count))

    def field_copy(ghost):
        return pltpu.make_async_remote_copy(src_ref=outgoing.at[ghost], dst_ref=held.at[row, path], send_sem=send_sem.at[ghost], recv_sem=recv_sem.at[path], device_id=field_target(ghost), device_id_type=MESH)

    def field_arrival(source):
        return pltpu.make_async_remote_copy(src_ref=outgoing.at[0], dst_ref=held.at[slab_id, source], send_sem=send_sem.at[0], recv_sem=recv_sem.at[source], device_id=(path, row), device_id_type=MESH)
    home_copy = pltpu.make_async_copy(outgoing.at[own], held.at[row, path], recv_sem.at[path])
    for load in loads[2:] + loads[:1]:
        load.wait()
    each = ghosts // PARTS
    turn_of = lax.rem(own, each)

    def send_plane(step):
        for turn in range(each):
            ghost = plane_at(SEND, step) * each + lax.rem(turn_of + turn, each)
            index = case[ghost] * SURF + pair[0, ghost]
            outgoing[ghost, 0] = field[0, index]
            outgoing[ghost, 1] = field[1, index]
            target_path, target_row = field_target(ghost)
            away = jnp.logical_or(ghost != own, jnp.logical_not(is_home))

            @pl.when(jnp.logical_and(away, order_of(target_path, target_row) > order))
            def _():
                pl.semaphore_wait(ready.at[target_path * row_count + target_row], 1)

            @pl.when(away)
            def _():
                field_copy(ghost).start()

            @pl.when(jnp.logical_not(away))
            def _():
                home_copy.start()

    def drain_plane(step, count):
        for turn in range(*count):
            ghost = plane_at(SEND, step) * each + lax.rem(turn_of + turn, each)

            @pl.when(jnp.logical_or(ghost != own, jnp.logical_not(is_home)))
            def _():
                field_copy(ghost).wait_send()
    for step in range(PARTS):
        send_plane(step)
    for turn in range(1, row_count):
        partner = chip * row_count + lax.rem(slab_id + turn, row_count)

        @pl.when(jnp.logical_and(lax.rem(partner, row_count) != row, order_of(partner, row) > order))
        def _():
            pl.semaphore_wait(ready.at[partner * row_count + row], 1)
    loads[1].wait()
    coefficient, power, gain = ghost_scalars(reflect, curvature, position, wave, pair, case, own)
    build_operator(cells, coefficient, power, table, spread, screened, both)

    def pass_copy(source, turn):
        return pltpu.make_async_remote_copy(src_ref=held.at[slab_id, source], dst_ref=held.at[slab_id, source], send_sem=pass_send.at[turn - 1, source], recv_sem=pass_recv.at[turn - 1, source], device_id=(chip * row_count + (slab_id + turn) % row_count, row), device_id_type=MESH)

    def pass_arrival(source, turn):
        return pltpu.make_async_remote_copy(src_ref=held.at[slab_id, source], dst_ref=held.at[(slab_id + row_count - turn) % row_count, source], send_sem=pass_send.at[turn - 1, source], recv_sem=pass_recv.at[turn - 1, source], device_id=(path, row), device_id_type=MESH)
    slab = pl.ds(pl.multiple_of(slab_id * slab_cells, slab_cells), slab_cells)

    def take_plane(step):
        for turn in range(group):
            source = plane_at(ARRIVE, step) * group + lax.rem(path + turn, group)

            @pl.when(jnp.logical_or(source != path, jnp.logical_not(is_home)))
            def _():
                field_arrival(source).wait_recv()

            @pl.when(jnp.logical_and(source == path, is_home))
            def _():
                home_copy.wait()
            for other in range(1, row_count):
                pass_copy(source, other).start()

    def first_plane(step):
        chunk = plane_at(ARRIVE, step)
        for turn in range(group):
            for other in range(1, row_count):
                pass_arrival(chunk * group + turn, other).wait_recv()

        def rows_of(part):
            return jnp.concatenate([held[side, pl.ds(chunk * group, group), part].reshape(tall, slab_cells) for side in range(row_count)], axis=1)
        rows = pl.ds(pl.multiple_of(chunk * tall, tall), tall)
        slab_first(rows_of(0), rows_of(1), slab, both, middle, rows)

    def half_at(index):
        return pl.ds(pl.multiple_of(index * (cells // 2), cells // 2), cells // 2)

    def half_second():

        @pl.loop(0, 2)
        def _(chunk):
            rows = half_at(chunk)
            real, imag = slab_second(both, middle, rows, half_at(plane // 2))
            partial[0, rows, :], partial[1, rows, :] = (real, imag)
    take_plane(0)
    take_plane(1)
    first_plane(0)
    first_plane(1)
    take_plane(2)
    half_second()
    first_plane(2)
    take_plane(3)
    first_plane(3)

    def bright_copies(target):
        return [pltpu.make_async_remote_copy(src_ref=source.at[target], dst_ref=arrived.at[own], send_sem=sent.at[target], recv_sem=received.at[own], device_id=(target, slab_id), device_id_type=MESH) for source, arrived, sent, received in ((bright, got, out_send, out_recv),)]

    def bright_arrivals(ghost):
        return [pltpu.make_async_remote_copy(src_ref=source.at[0], dst_ref=arrived.at[ghost], send_sem=sent.at[0], recv_sem=received.at[ghost], device_id=(path, row), device_id_type=MESH) for source, arrived, sent, received in ((bright, got, out_send, out_recv),)]
    home_bright = [pltpu.make_async_copy(bright.at[path], got.at[own], out_recv.at[own])]
    unit = gain * gain * (CASES / ghosts)
    few = group // 2
    for turned in range(2 * PARTS):
        first = plane_at(BACK, turned // 2) * group + turned % 2 * few
        rows = pl.ds(pl.multiple_of(first * piece, few * piece), few * piece)
        real, imag = slab_second(both, middle, rows, half_at(1 - plane // 2))
        real, imag = (real + partial[0, rows, :], imag + partial[1, rows, :])
        intensity = (real * real + imag * imag).reshape(few, piece, slab_cells)
        bright[pl.ds(first, few)] = encode(intensity * unit)
        for step in range(few):
            target = first + lax.rem(path + step, few)

            @pl.when(jnp.logical_or(target != path, jnp.logical_not(is_home)))
            def _():
                for copy in bright_copies(target):
                    copy.start()

            @pl.when(jnp.logical_and(target == path, is_home))
            def _():
                for copy in home_bright:
                    copy.start()
    out[...] = jnp.zeros_like(out)
    for step in range(PARTS):
        drain_plane(step, (0, each))
    for source in range(paths):
        for turn in range(1, row_count):
            pass_copy(source, turn).wait_send()

    def drain_back(step):
        for turn in range(group):
            target = plane_at(BACK, step) * group + lax.rem(path + turn, group)

            @pl.when(jnp.logical_or(target != path, jnp.logical_not(is_home)))
            def _():
                for copy in bright_copies(target):
                    copy.wait_send()
    for step in range(ghosts):
        if step == ghosts - each:
            drain_back(0)
            drain_back(1)
        ghost = plane_at(ARRIVE, step // each) * each + lax.rem(turn_of + step, each)

        @pl.when(jnp.logical_or(ghost != own, jnp.logical_not(is_home)))
        def _():
            for copy in bright_arrivals(ghost):
                copy.wait_recv()

        @pl.when(jnp.logical_and(ghost == own, is_home))
        def _():
            for copy in home_bright:
                copy.wait()
        values = decode(got[ghost])
        for index in range(CASES):
            chosen = jnp.where(case[ghost] == index, 1.0, 0.0)
            out[index] += chosen * values
    for step in range(2, PARTS):
        drain_back(step)


def whole(cells, paths, row_count, main_field, table, *small):
    ghosts = small[-1].shape[0]
    piece, slab_cells = (cells // paths, cells // row_count)
    return pl.pallas_call(functools.partial(whole_kernel, cells, paths, row_count), out_shape=jax.ShapeDtypeStruct((CASES, piece, slab_cells), F32), in_specs=[pl.BlockSpec(memory_space=pltpu.HBM)] * 8, out_specs=VMEM, scratch_shapes=scratch_of(cells, slab_cells) + [pltpu.VMEM(main_field.shape, BF16), pltpu.VMEM((2, cells, cells), BF16), *[pltpu.SMEM(array.shape, array.dtype) for array in small], pltpu.VMEM((ghosts, 2, piece, slab_cells), BF16), pltpu.VMEM((row_count, paths, 2, piece, slab_cells), BF16), pltpu.VMEM((2, cells, slab_cells), F32), pltpu.VMEM((paths, piece, slab_cells), jnp.int16), pltpu.VMEM((ghosts, piece, slab_cells), jnp.int16), pltpu.SemaphoreType.DMA((8,)), pltpu.SemaphoreType.DMA((ghosts,)), pltpu.SemaphoreType.DMA((paths,)), pltpu.SemaphoreType.DMA((row_count - 1, paths)), pltpu.SemaphoreType.DMA((row_count - 1, paths)), pltpu.SemaphoreType.DMA((paths,)), pltpu.SemaphoreType.DMA((ghosts,)), pltpu.SemaphoreType.REGULAR((paths * row_count,))], compiler_params=pltpu.CompilerParams(collective_id=0, has_side_effects=True, vmem_limit_bytes=60 * 1024 * 1024))(main_field, table, *small)


def slab_kernel(cells, row_count, field, table, reflect, curvature, position, wave, pair, case, slot, out, spread, screened, both, middle):
    slab_cells = cells // row_count
    coefficient, power, gain = ghost_scalars(reflect, curvature, position, wave, pair, case, slot[0])
    build_operator(cells, coefficient, power, table, spread, screened, both)
    slab = pl.ds(pl.multiple_of(slot[1] * slab_cells, slab_cells), slab_cells)
    tall = cells // 2

    @pl.loop(0, 2)
    def _(chunk):
        rows = pl.ds(pl.multiple_of(chunk * tall, tall), tall)
        slab_first(field[0, rows, :], field[1, rows, :], slab, both, middle, rows)

    @pl.loop(0, 2)
    def _(chunk):
        rows = pl.ds(pl.multiple_of(chunk * tall, tall), tall)
        real, imag = slab_second(both, middle, rows, pl.ds(0, cells))
        out[rows, :] = gain * gain * (real * real + imag * imag)


def local(main_field, table, *small):
    paths = lax.axis_size('path')
    row_count = lax.axis_size('row')
    piece, slab_cells = main_field.shape[2:]
    cells = piece * paths
    pair, case = small[-2:]
    ghosts = case.shape[0]
    if piece % 16 == 0 and ghosts == paths and (paths % (PARTS * row_count) == 0) and (row_count > 1):
        return whole(cells, paths, row_count, main_field, table, *small)
    per_device = ghosts // paths
    fields = jnp.arange(main_field.shape[1], dtype=jnp.int32)
    wanted = (fields[None, :] == (case * SURF + pair[0])[:, None]).astype(BF16)
    picked = jnp.einsum('gf,cfrv->cgrv', wanted, main_field, preferred_element_type=F32).astype(BF16)
    picked = picked.reshape(2, paths, per_device, piece, slab_cells)
    arrived = lax.all_to_all(picked, 'path', split_axis=1, concat_axis=3, tiled=True)
    fields = lax.all_gather(arrived.reshape(2, per_device, cells, slab_cells), 'row', axis=3, tiled=True)
    bright = []
    for index in range(per_device):
        slot = jnp.stack([lax.axis_index('path') * per_device + index, lax.axis_index('row')])
        bright.append(pl.pallas_call(functools.partial(slab_kernel, cells, row_count), out_shape=jax.ShapeDtypeStruct((cells, slab_cells), F32), in_specs=[VMEM, VMEM] + [SMEM] * 7, out_specs=VMEM, scratch_shapes=scratch_of(cells, slab_cells), compiler_params=pltpu.CompilerParams(vmem_limit_bytes=48 * 1024 * 1024))(fields[:, index], table, *small, slot))
    got = lax.all_to_all(jnp.stack(bright), 'path', split_axis=1, concat_axis=0, tiled=True)
    got = got.reshape(paths, per_device, piece, slab_cells).reshape(ghosts, piece, slab_cells)
    chosen = (case[:, None] == jnp.arange(CASES, dtype=jnp.int32)).astype(F32)
    total = jnp.sum(chosen[:, :, None, None] * got[:, None], 0)
    return total * (CASES / ghosts)


def solution(mesh):
    in_specs = (P(None, None, 'path', 'row'), P(), P(), P(), P(), P(), P())
    out_specs = P(None, 'path', 'row')

    def run(main_field, reflect, curvature, position, wave, pair, case):
        small = (reflect, curvature, position, wave, pair.T, case)
        table = cosine_table(main_field.shape[2] * mesh.shape['path'])
        return local(main_field, jnp.asarray(table), *small)
    return jax.shard_map(run, mesh=mesh, in_specs=in_specs, out_specs=out_specs, check_vma=False)
```
